512 devices in a mesh: lon: 16 (over z), lat: 8 (over y, core), tp: 4 (over x).
Axes of the slice: x: 4, y: 4, z: 16, core: 2. Of those that a mesh axis runs over, the one named last changes fastest.
Arguments:
- features: bfloat16 [8, 2048, 2048], P('lat', 'lon', 'tp'), may hold values from -6 to 6
- projections: bfloat16 [8, 2048, 256], P('lat', 'lon'), may hold values from -6 to 6
- step_raw: float32 [8, 2048, 32], P('lat', 'lon', 'tp'), may hold values from -4 to 4
- step_bias: float32 [32], P('tp'), may hold values from -1 to 0.5
- decay_log: float32 [2, 32], P(None, 'tp'), may hold values from -8.5 to -2.3
- skip_gain: float32 [32], P('tp'), may hold values from 0.5 to 1.5
- conv_features: float32 [9, 2048], P(None, 'tp'), may hold values from -2 to 2
- conv_projections: float32 [9, 256], replicated, may hold values from -0.25 to 0.25
- state_east: float32 [8, 32, 64, 128], P('lat', 'tp'), may hold values from -6 to 6
- state_west: float32 [8, 32, 64, 128], P('lat', 'tp'), may hold values from -6 to 6
- cotangent: bfloat16 [8, 2048, 2048], P('lat', 'lon', 'tp'), may hold values from -6 to 6
Outputs:
- mixed: bfloat16 [8, 2048, 2048], P('lat', 'lon', 'tp')
- grad_features: bfloat16 [8, 2048, 2048], P('lat', 'lon', 'tp')
- grad_projections: bfloat16 [8, 2048, 256], P('lat', 'lon')
- grad_step: float32 [8, 2048, 32], P('lat', 'lon', 'tp')
- grad_conv_features: float32 [9, 2048], P(None, 'tp')
- grad_conv_projections: float32 [9, 256], replicated
- grad_decay_log: float32 [2, 32], P(None, 'tp')
- grad_step_bias: float32 [32], P('tp')
- grad_skip_gain: float32 [32], P('tp')
The draws below stay inside these ranges and needn't reach their ends.
All inputs are finite; a program needn't handle non-finite values.
Results may differ from the reference program's by a relative error of at most 0.0065.
Values may be sent and summed in bfloat16 or wider, within the bound.
A program may use at most 128 MiB of HBM per device.

```python
import jax
import jax.numpy as jnp
from jax import lax

H = 32
P_SIZE = 64
N = 128
COLS_DEV = 128
NR = 8
NC = 2048


def shard_levels(stream_key, extent, cuts, smallest, top_value):
    level, own = 1.0, jax.random.fold_in(stream_key, 6)
    for dim, blocks in cuts:
        draws = jnp.exp(jax.random.uniform(jax.random.fold_in(own, dim), (blocks,), jnp.float32, smallest / len(cuts), top_value / len(cuts)))
        level = level * jnp.repeat(draws, extent[dim] // blocks).reshape([-1 if axis == dim else 1 for axis in range(len(extent))])
    return level


def noise(stream_key, extent, deviation, reach, cuts=(), kind=jnp.bfloat16):
    drawn = jax.random.normal(stream_key, extent, jnp.float32) * deviation
    if len(cuts) > 0:
        drawn = shard_levels(stream_key, extent, cuts, -0.22, 0.18) * drawn
    return jnp.clip(drawn, min=-reach, max=reach).astype(kind)


def setup_inputs(seed: int = 0) -> dict:
    keys = jax.random.split(jax.random.key(seed), 12)
    return {
        "features": noise(keys[0], (NR, NC, H * P_SIZE), 1.0, 6.0, ((0, 8), (1, 16), (2, 4))),
        "projections": noise(keys[1], (NR, NC, 2 * N), 1.0, 6.0, ((0, 8), (1, 16))),
        "step_raw": noise(keys[2], (NR, NC, H), 1.0, 4.0, ((0, 8), (1, 16), (2, 4)), jnp.float32),
        "step_bias": jnp.clip(-1.0 + 1.5 * jax.random.uniform(keys[3], (H,), jnp.float32) ** shard_levels(keys[3], (H,), ((0, 4),), -0.2, 0.2), -1.0, 0.5),
        "decay_log": jnp.clip(-8.5 + 6.2 * jax.random.uniform(keys[4], (2, H), jnp.float32) ** shard_levels(keys[4], (2, H), ((1, 4),), -0.2, 0.2), -8.5, -2.3),
        "skip_gain": jnp.clip(0.5 + 1.0 * jax.random.uniform(keys[5], (H,), jnp.float32) ** shard_levels(keys[5], (H,), ((0, 4),), -0.2, 0.2), 0.5, 1.5),
        "conv_features": noise(keys[6], (9, H * P_SIZE), 9 ** -0.5, 2.0, ((1, 4),), jnp.float32),
        "conv_projections": noise(keys[7], (9, 2 * N), 576 ** -0.5, 0.25, (), jnp.float32),
        "state_east": noise(keys[8], (NR, H, P_SIZE, N), 1.0, 6.0, ((0, 8), (1, 4)), jnp.float32),
        "state_west": noise(keys[9], (NR, H, P_SIZE, N), 1.0, 6.0, ((0, 8), (1, 4)), jnp.float32),
        "cotangent": noise(keys[10], (NR, NC, H * P_SIZE), 1.0, 6.0, ((0, 8), (1, 16), (2, 4))),
    }


PRECISE = lax.Precision.HIGHEST

def log_decay(step_sizes, rates):
    return jnp.cumsum(-step_sizes * rates, axis=1)

def block_ends(inner, b_part, step_sizes, rates):
    decay_sum = log_decay(step_sizes, rates)
    closing = decay_sum[:, -1:, :]
    factor = jnp.exp(closing - decay_sum) * step_sizes
    scaled = factor[..., None] * inner
    summed = jnp.einsum('rjhp,rjn->rhpn', scaled, b_part, precision=PRECISE)
    return (jnp.exp(closing[:, 0, :]), summed)

def head_mix(inner_head, scores, decay_head, steps_head):
    count = scores.shape[1]
    causal = lax.broadcasted_iota(jnp.int32, (count, count), 0) >= lax.broadcasted_iota(jnp.int32, (count, count), 1)
    spread = jnp.where(causal, decay_head[:, :, None] - decay_head[:, None, :], 0.0)
    mixing = jnp.where(causal, jnp.exp(spread), 0.0) * scores * steps_head[:, None, :]
    return jnp.einsum('rij,rjp->rip', mixing, inner_head, precision=PRECISE)

def block_mix(inner, b_part, c_part, step_sizes, rates):
    decay_sum = log_decay(step_sizes, rates)
    scores = jnp.einsum('rin,rjn->rij', c_part, b_part, precision=PRECISE)
    mixer = jax.checkpoint(head_mix)
    results = [mixer(inner[:, :, member, :], scores, decay_sum[:, :, member], step_sizes[:, :, member]) for member in range(inner.shape[2])]
    return jnp.stack(results, axis=2)

def block_reads(c_part, step_sizes, rates, entering):
    decay_sum = log_decay(step_sizes, rates)
    reading = jnp.einsum('rin,rhpn->rihp', c_part, entering, precision=PRECISE)
    return reading * jnp.exp(decay_sum)[..., None]

def stencil(padded, kernel, row_count, col_count):
    total = jnp.zeros((row_count, col_count, padded.shape[2]), jnp.float32)
    for offset_row in range(3):
        for offset_col in range(3):
            total = total + kernel[3 * offset_row + offset_col] * padded[offset_row:offset_row + row_count, offset_col:offset_col + col_count].astype(jnp.float32)
    return total

def stencil_adjoint(padded, kernel, row_count, col_count):
    total = jnp.zeros((row_count, col_count, padded.shape[2]), jnp.float32)
    for offset_row in range(3):
        for offset_col in range(3):
            total = total + kernel[3 * offset_row + offset_col] * padded[2 - offset_row:2 - offset_row + row_count, 2 - offset_col:2 - offset_col + col_count].astype(jnp.float32)
    return total

def stencil_weights(grads, padded, row_count, col_count):
    grads32 = grads.astype(jnp.float32)
    rows_out = []
    for offset_row in range(3):
        for offset_col in range(3):
            window = padded[offset_row:offset_row + row_count, offset_col:offset_col + col_count].astype(jnp.float32)
            rows_out.append(lax.optimization_barrier(jnp.sum(grads32 * window, axis=(0, 1))))
    return jnp.stack(rows_out)

def direction(inner, b_part, c_part, step_sizes, rates, initial):
    count = inner.shape[1] // COLS_DEV

    def split(array):
        return jnp.moveaxis(array.reshape((array.shape[0], count, COLS_DEV) + array.shape[2:]), 1, 0)

    def advance(carry, pieces):
        inner_b, b_b, c_b, steps_b = pieces
        mix = block_mix(inner_b, b_b, c_b, steps_b, rates)
        reading = block_reads(c_b, steps_b, rates, carry)
        closing, summed = block_ends(inner_b, b_b, steps_b, rates)
        return (closing[..., None, None] * carry + summed, mix + reading)
    final_state, results = lax.scan(jax.checkpoint(advance), initial, (split(inner), split(b_part), split(c_part), split(step_sizes)))
    return jnp.moveaxis(results, 0, 1).reshape(inner.shape)

def reference(features, projections, step_raw, step_bias, decay_log, skip_gain, conv_features, conv_projections, state_east, state_west, cotangent):
    row_count, col_count, width = features.shape
    heads = step_raw.shape[2]
    head_size = width // heads
    state_size = projections.shape[2] // 2
    joined = jnp.concatenate([features, projections], axis=2)
    kernel = jnp.concatenate([conv_features, conv_projections], axis=1)
    padded = jnp.pad(joined, ((1, 1), (1, 1), (0, 0)))
    before = stencil(padded, kernel, row_count, col_count)
    active = jax.nn.silu(before).astype(jnp.bfloat16)
    inner32 = active[:, :, :width].astype(jnp.float32).reshape(row_count, col_count, heads, head_size)
    proj32 = active[:, :, width:].astype(jnp.float32)

    def forward(inner, proj, raw, bias, logs, gain):
        step_sizes = jax.nn.softplus(raw + bias)
        rates = jnp.exp(logs)
        b_part = proj[:, :, :state_size]
        c_part = proj[:, :, state_size:]
        east = direction(inner, b_part, c_part, step_sizes, rates[0], state_east)
        west = direction(jnp.flip(inner, 1), jnp.flip(b_part, 1), jnp.flip(c_part, 1), jnp.flip(step_sizes, 1), rates[1], state_west)
        return east + jnp.flip(west, 1) + gain[:, None] * inner
    mixed32, pullback = jax.vjp(forward, inner32, proj32, step_raw, step_bias, decay_log, skip_gain)
    grads = pullback(cotangent.reshape(row_count, col_count, heads, head_size).astype(jnp.float32))
    mixed = mixed32.reshape(row_count, col_count, width).astype(jnp.bfloat16)
    g_active = jnp.concatenate([grads[0].reshape(row_count, col_count, width).astype(jnp.bfloat16), grads[1].astype(jnp.bfloat16)], axis=2)
    slope = jax.nn.sigmoid(before)
    g_before = (g_active.astype(jnp.float32) * slope * (1.0 + before * (1.0 - slope))).astype(jnp.bfloat16)
    g_padded = jnp.pad(g_before, ((1, 1), (1, 1), (0, 0)))
    g_joined = stencil_adjoint(g_padded, kernel, row_count, col_count)
    g_kernel = stencil_weights(g_before, padded, row_count, col_count)
    scale = (row_count * col_count) ** (-0.5)
    return (mixed, g_joined[:, :, :width].astype(jnp.bfloat16), g_joined[:, :, width:].astype(jnp.bfloat16), grads[2], g_kernel[:, :width] * scale, g_kernel[:, width:] * scale, grads[4] * scale, grads[3] * scale, grads[5] * scale)
```

```python
from functools import partial

import jax
import jax.numpy as jnp
from jax import lax
from jax.experimental import pallas as pl
from jax.experimental.pallas import tpu as pltpu
from jax.sharding import PartitionSpec as P

MESH = pl.DeviceIdType.MESH
F32 = jnp.float32
BF16 = jnp.bfloat16
T = 128
EXT = T + 16
EDGES = ((0, -1), (0, 1), (-1, -1), (-1, 1), (1, -1), (1, 1))


def hi(a, b):
    return jnp.dot(a, b, precision=lax.Precision.HIGHEST, preferred_element_type=F32)


def nn(a, b):
    return jnp.dot(a, b, preferred_element_type=F32)


def nt(a, b):
    return lax.dot_general(a, b, (((1,), (1,)), ((), ())), preferred_element_type=F32)


def tn(a, b):
    return lax.dot_general(a, b, (((0,), (0,)), ((), ())), preferred_element_type=F32)


def grid_peer(d_lat, d_lon):
    lat_n, lon_n = lax.axis_size("lat"), lax.axis_size("lon")
    return {
        "lat": lax.rem(lax.axis_index("lat") + d_lat + lat_n, lat_n),
        "lon": lax.rem(lax.axis_index("lon") + d_lon + lon_n, lon_n),
    }


def greet(peers):
    barrier = pltpu.get_barrier_semaphore()
    for peer in peers:
        pl.semaphore_signal(barrier, inc=1, device_id=peer, device_id_type=MESH)
    pl.semaphore_wait(barrier, len(peers))


def grid_peers():
    return [grid_peer(a, b) for a in (-1, 0, 1) for b in (-1, 0, 1) if (a, b) != (0, 0)]


def halo_copies(src, rows, edges, send, recv):
    copies = []
    for slot, a in enumerate((-1, 1)):
        copies.append(
            pltpu.make_async_remote_copy(
                src, rows.at[slot], send.at[slot], recv.at[slot],
                device_id=grid_peer(-a, 0), device_id_type=MESH,
            )
        )
    for slot, (a, b) in enumerate(EDGES):
        part = src.at[pl.ds(T - 16, 16)] if b < 0 else src.at[pl.ds(0, 16)]
        copies.append(
            pltpu.make_async_remote_copy(
                part, edges.at[slot], send.at[2 + slot], recv.at[2 + slot],
                device_id=grid_peer(-a, -b), device_id_type=MESH,
            )
        )
    return copies


def fill_extended(src, rows, edges, ext):
    lat, lon = lax.axis_index("lat"), lax.axis_index("lon")
    lat_n, lon_n = lax.axis_size("lat"), lax.axis_size("lon")
    keep = {
        (1, -1): (lat > 0).astype(F32),
        (1, 1): (lat < lat_n - 1).astype(F32),
        (2, -1): (lon > 0).astype(F32),
        (2, 1): (lon < lon_n - 1).astype(F32),
    }
    ext[1, 8 : 8 + T] = src[...].astype(F32)
    ext[0, 8 : 8 + T] = rows[0].astype(F32) * keep[1, -1]
    ext[2, 8 : 8 + T] = rows[1].astype(F32) * keep[1, 1]
    for slot, (a, b) in enumerate(EDGES):
        scale = keep[2, b] if a == 0 else keep[2, b] * keep[1, a]
        tile = edges[slot].astype(F32) * scale
        if b < 0:
            ext[a + 1, 0:8] = tile[8:16]
        else:
            ext[a + 1, 8 + T :] = tile[0:8]


def stencil(ext, taps, lanes, adjoint):
    sums = []
    for b in range(3):
        total = None
        for a in range(3):
            term = taps[3 * a + b : 3 * a + b + 1, lanes] * ext[2 - a if adjoint else a, :, lanes]
            total = term if total is None else total + term
        sums.append(total)
    west, east = (sums[2], sums[0]) if adjoint else (sums[0], sums[2])
    full = pltpu.roll(west, 1, 0) + sums[1] + pltpu.roll(east, EXT - 1, 0)
    return full[8 : 8 + T]


def conv_kernel(joined, taps, before, active, ext, rows, edges, send, recv):
    greet(grid_peers())
    copies = halo_copies(joined, rows, edges, send, recv)
    for copy in copies:
        copy.start()
    for copy in copies:
        copy.wait()
    fill_extended(joined, rows, edges, ext)
    for part in range(joined.shape[1] // 128):
        lanes = slice(128 * part, 128 * part + 128)
        value = stencil(ext, taps, lanes, False)
        before[:, lanes] = value
        active[:, lanes] = (value * jax.nn.sigmoid(value)).astype(BF16)


def adjoint_kernel(grad, taps, out_f, out_p, ext, rows, edges, send, recv):
    greet(grid_peers())
    copies = halo_copies(grad, rows, edges, send, recv)
    for copy in copies:
        copy.start()
    for copy in copies:
        copy.wait()
    fill_extended(grad, rows, edges, ext)
    width = out_f.shape[1]
    for part in range(grad.shape[1] // 128):
        lanes = slice(128 * part, 128 * part + 128)
        value = stencil(ext, taps, lanes, True).astype(BF16)
        if 128 * part < width:
            out_f[:, lanes] = value
        else:
            out_p[:, 128 * part - width : 128 * part - width + 128] = value


def state_kernel(
    active, before, ext, cot, raw_c, raw_r, bias_r, bias_c, logs_r, logs_c, gain, start_e, start_w,
    mixed, grad_before, grad_step, params,
    add_r, add_l, in_r, in_l, out_r, out_l, dec_r, dec_l, cols, gathered,
    send_r, recv_r, send_l, recv_l, send_t, recv_t,
):
    lon, tp = lax.axis_index("lon"), lax.axis_index("tp")
    lon_n, tp_n = lax.axis_size("lon"), lax.axis_size("tp")
    heads = raw_c.shape[1]
    width = cot.shape[1]
    size = width // heads
    chunks = 2 * heads
    tp_peers = [{"tp": lax.rem(tp + d, tp_n)} for d in range(1, tp_n)]
    greet([grid_peer(0, -1), grid_peer(0, 1)] + tp_peers)

    row_i = lax.broadcasted_iota(jnp.int32, (T, T), 0)
    col_i = lax.broadcasted_iota(jnp.int32, (T, T), 1)
    lower = (row_i >= col_i).astype(F32)
    upper = (row_i <= col_i).astype(F32)
    spread = (
        lax.broadcasted_iota(jnp.int32, (heads, width), 1) // size
        == lax.broadcasted_iota(jnp.int32, (heads, width), 0)
    ).astype(F32)
    gather = (
        lax.broadcasted_iota(jnp.int32, (width, heads), 0) // size
        == lax.broadcasted_iota(jnp.int32, (width, heads), 1)
    ).astype(F32)

    def softplus(v):
        return jnp.maximum(v, 0.0) + jnp.log1p(jnp.exp(-jnp.abs(v)))

    shifted = raw_c[...] + bias_r[...]
    steps = softplus(shifted)
    steps_r = softplus(raw_r[...] + bias_c[...])
    rate_e, rate_w = jnp.exp(logs_r[0:1]), jnp.exp(logs_r[1:2])
    rates_c = jnp.exp(logs_c[...])
    sum_e = hi(lower, -steps * rate_e)
    sum_w = hi(upper, -steps * rate_w)
    sum_er = hi(-steps_r * rates_c[:, 0:1], upper)
    sum_wr = hi(-steps_r * rates_c[:, 1:2], lower)
    tot_e, tot_w = sum_e[T - 1 : T], sum_w[0:1]
    far_e, far_w = jnp.exp(tot_e - sum_e), jnp.exp(tot_w - sum_w)
    fac_e, fac_w = far_e * steps, far_w * steps
    wide_ee, wide_ew = hi(jnp.exp(sum_e), spread), hi(jnp.exp(sum_w), spread)
    wide_fe, wide_fw = hi(fac_e, spread), hi(fac_w, spread)
    close_e = jnp.broadcast_to(jnp.exp(sum_er[:, T - 1 : T]), (heads, T))
    close_w = jnp.broadcast_to(jnp.exp(sum_wr[:, 0:1]), (heads, T))
    dec_r[0:heads] = close_e
    dec_r[heads:chunks] = close_w
    dec_l[0:heads] = close_w
    dec_l[heads:chunks] = close_e

    inner = active[:, 0:width].astype(F32)
    b_part = active[:, width : width + T]
    c_part = active[:, width + T : width + 2 * T]
    incoming = cot[...].astype(F32)
    src_e, src_w = (inner * wide_fe).astype(BF16), (inner * wide_fw).astype(BF16)
    inc_e, inc_w = (incoming * wide_ee).astype(BF16), (incoming * wide_ew).astype(BF16)
    shape3 = (heads, size, T)
    add_r[0:heads] = tn(src_e, b_part).reshape(shape3)
    add_r[heads:chunks] = tn(inc_w, c_part).reshape(shape3)
    add_l[0:heads] = tn(src_w, b_part).reshape(shape3)
    add_l[heads:chunks] = tn(inc_e, c_part).reshape(shape3)

    @pl.when(lon == 0)
    def _():
        in_r[0:heads] = start_e[...].reshape(shape3)
        in_r[heads:chunks] = jnp.zeros(shape3, F32)

    @pl.when(lon == lon_n - 1)
    def _():
        in_l[0:heads] = start_w[...].reshape(shape3)
        in_l[heads:chunks] = jnp.zeros(shape3, F32)

    def copy_r(q):
        return pltpu.make_async_remote_copy(
            out_r.at[q], in_r.at[q], send_r.at[q], recv_r.at[q],
            device_id=grid_peer(0, 1), device_id_type=MESH,
        )

    def copy_l(q):
        return pltpu.make_async_remote_copy(
            out_l.at[q], in_l.at[q], send_l.at[q], recv_l.at[q],
            device_id=grid_peer(0, -1), device_id_type=MESH,
        )

    lead = 3
    skew_r = jnp.maximum(0, (2 * lon - (lon_n - 1)) * lead)
    skew_l = jnp.maximum(0, ((lon_n - 1) - 2 * lon) * lead)

    def hop(slot, _):
        q_r, q_l = slot - skew_r, slot - skew_l

        @pl.when((q_r >= 0) & (q_r < chunks))
        def _():
            @pl.when(lon > 0)
            def _():
                copy_r(q_r).wait_recv()

            @pl.when(lon < lon_n - 1)
            def _():
                out_r[q_r] = dec_r[pl.ds(q_r, 1), :] * in_r[q_r] + add_r[q_r]
                copy_r(q_r).start()

        @pl.when((q_l >= 0) & (q_l < chunks))
        def _():
            @pl.when(lon < lon_n - 1)
            def _():
                copy_l(q_l).wait_recv()

            @pl.when(lon > 0)
            def _():
                out_l[q_l] = dec_l[pl.ds(q_l, 1), :] * in_l[q_l] + add_l[q_l]
                copy_l(q_l).start()

        return 0

    lax.fori_loop(0, chunks + lead * (lon_n - 1), hop, 0)

    scores = nt(c_part, b_part)
    head_i = lax.broadcasted_iota(jnp.int32, (T, heads), 1)
    lane_half = lax.broadcasted_iota(jnp.int32, (T, T), 1) // size
    row_l = jnp.zeros((T, heads), F32)
    row_u = jnp.zeros((T, heads), F32)
    grad_scores = jnp.zeros((T, T), F32)
    per = T // size
    mixes, pulls = [], []
    for pair in range(heads // per):
        lanes = slice(T * pair, T * pair + T)
        inner_p, incoming_p = inner[:, lanes], incoming[:, lanes]
        mix, pull = None, None
        for member in range(per):
            h = per * pair + member
            mine = (lane_half == member).astype(F32)
            inner_m = (inner_p * mine).astype(BF16)
            incoming_m = (incoming_p * mine).astype(BF16)
            gap = jnp.where(
                row_i >= col_i,
                sum_e[:, h : h + 1] - sum_er[h : h + 1],
                sum_w[:, h : h + 1] - sum_wr[h : h + 1],
            )
            decay = jnp.where(row_i == col_i, 2.0, jnp.exp(gap)) * steps_r[h : h + 1]
            grad_mix = nt(incoming_m, inner_m) * decay
            grad_scores = grad_scores + grad_mix
            weight = grad_mix * scores
            below = jnp.where(row_i > col_i, weight, 0.0)
            above = jnp.where(row_i < col_i, weight, 0.0)
            row_l = jnp.where(head_i == h, jnp.sum(below, axis=1, keepdims=True), row_l)
            row_u = jnp.where(head_i == h, jnp.sum(above, axis=1, keepdims=True), row_u)
            cols[0, h : h + 1] = jnp.sum(below, axis=0, keepdims=True)
            cols[1, h : h + 1] = jnp.sum(above, axis=0, keepdims=True)
            cols[2, h : h + 1] = jnp.sum(weight, axis=0, keepdims=True)
            mixing = (decay * scores).astype(BF16)
            y, g = nn(mixing, inner_m), tn(mixing, incoming_m)
            mix = y if mix is None else mix + y
            pull = g if pull is None else pull + g
        mixes.append(mix)
        pulls.append(pull)
    grad_inner = jnp.concatenate(pulls, axis=1)
    total = jnp.concatenate(mixes, axis=1)

    def settle(q, _):
        @pl.when(lon < lon_n - 1)
        def _():
            copy_r(q).wait_send()

        @pl.when(lon > 0)
        def _():
            copy_l(q).wait_send()

        return 0

    lax.fori_loop(0, chunks, settle, 0)

    flat = (width, T)
    ent_e, adj_w = in_r[0:heads].reshape(flat), in_r[heads:chunks].reshape(flat)
    ent_w, adj_e = in_l[0:heads].reshape(flat), in_l[heads:chunks].reshape(flat)
    ent_eb, ent_wb = ent_e.astype(BF16), ent_w.astype(BF16)
    adj_eb, adj_wb = adj_e.astype(BF16), adj_w.astype(BF16)

    scores_b = grad_scores.astype(BF16)
    me = pl.ds(tp, 1)
    grad_b = tn(scores_b, c_part) + nn(src_e, adj_eb) + nn(src_w, adj_wb)
    grad_c = nn(scores_b, b_part) + nn(inc_e, ent_eb) + nn(inc_w, ent_wb)
    gathered[me, :, 0:T] = grad_b[None]
    gathered[me, :, T : 2 * T] = grad_c[None]
    copies = [
        pltpu.make_async_remote_copy(
            gathered.at[tp], gathered.at[tp], send_t.at[d], recv_t.at[d],
            device_id=peer, device_id_type=MESH,
        )
        for d, peer in enumerate(tp_peers)
    ]
    for copy in copies:
        copy.start()

    read_e = nt(c_part, ent_eb) * wide_ee
    read_w = nt(c_part, ent_wb) * wide_ew
    pull_e, pull_w = nt(b_part, adj_eb), nt(b_part, adj_wb)
    mixed[...] = (total + read_e + read_w + gain[...] * inner).astype(BF16)
    grad_inner = grad_inner + wide_fe * pull_e + wide_fw * pull_w + gain[...] * incoming
    r_e, r_w = hi(read_e * incoming, gather), hi(read_w * incoming, gather)
    q_e, q_w = hi(pull_e * inner, gather), hi(pull_w * inner, gather)
    ones = jnp.ones((8, T), F32)

    def per_head(v):
        return lax.dot_general(
            ones, hi(spread, v), (((1,), (1,)), ((), ())),
            precision=lax.Precision.HIGHEST, preferred_element_type=F32,
        )[0:1]

    end_e, end_w = per_head(adj_e * ent_e), per_head(adj_w * ent_w)
    w_e, w_w = fac_e * q_e, fac_w * q_w
    const_e = jnp.sum(w_e, axis=0, keepdims=True) + jnp.exp(tot_e) * end_e
    const_w = jnp.sum(w_w, axis=0, keepdims=True) + jnp.exp(tot_w) * end_w
    grad_log_e = hi(upper, row_l - cols[0].T + r_e - w_e) + const_e
    grad_log_w = hi(lower, row_u - cols[1].T + r_w - w_w) + const_w
    grad_steps = (
        (cols[2] / steps_r).T + far_e * q_e + far_w * q_w - rate_e * grad_log_e - rate_w * grad_log_w
    )
    grad_raw = grad_steps * jax.nn.sigmoid(shifted)
    grad_step[...] = grad_raw
    params[...] = jnp.zeros(params.shape, F32)
    params[9:10, 0:heads] = jnp.sum(-steps * rate_e * grad_log_e, axis=0, keepdims=True)
    params[10:11, 0:heads] = jnp.sum(-steps * rate_w * grad_log_w, axis=0, keepdims=True)
    params[11:12, 0:heads] = jnp.sum(grad_raw, axis=0, keepdims=True)
    params[12:13, 0:heads] = jnp.sum(hi(incoming * inner, gather), axis=0, keepdims=True)

    def back(lanes, grad_active):
        value = before[:, lanes]
        slope = jax.nn.sigmoid(value)
        grad = (
            grad_active.astype(BF16).astype(F32) * slope * (1.0 + value * (1.0 - slope))
        ).astype(BF16)
        grad_before[:, lanes] = grad
        edge = jnp.zeros((8, 128), F32)
        wide = jnp.concatenate([edge, grad.astype(F32), edge], axis=0)
        for b in range(3):
            moved = wide if b == 1 else pltpu.roll(wide, EXT - 1 if b == 0 else 1, 0)
            for a in range(3):
                params[3 * a + b : 3 * a + b + 1, lanes] = jnp.sum(
                    moved * ext[a, :, lanes], axis=0, keepdims=True
                )

    for part in range(width // 128):
        lanes = slice(128 * part, 128 * part + 128)
        back(lanes, grad_inner[:, lanes])
    for copy in copies:
        copy.wait()
    proj = gathered[0]
    for d in range(1, tp_n):
        proj = proj + gathered[d]
    for part in range(2):
        back(slice(width + 128 * part, width + 128 * part + 128), proj[:, 128 * part : 128 * part + 128])


VM = pl.BlockSpec(memory_space=pltpu.VMEM)


def call(kernel, outs, scratch, ident, ins):
    return pl.pallas_call(
        kernel,
        out_shape=outs,
        in_specs=[VM] * len(ins),
        out_specs=tuple(VM for _ in outs),
        scratch_shapes=scratch,
        compiler_params=pltpu.CompilerParams(
            collective_id=ident, has_side_effects=True, vmem_limit_bytes=60 << 20
        ),
    )(*ins)


def shards(
    features, projections, step_raw, step_bias, decay_log, skip_gain, conv_features,
    conv_projections, state_east, state_west, cotangent,
):
    width, heads = features.shape[2], step_raw.shape[2]
    both = width + projections.shape[2]
    tp_n = lax.axis_size("tp")
    sds = jax.ShapeDtypeStruct
    dma = pltpu.SemaphoreType.DMA
    joined = jnp.concatenate([features[0], projections[0]], axis=1)
    taps = jnp.concatenate([conv_features, conv_projections], axis=1)
    halo = [
        pltpu.VMEM((2, T, both), BF16),
        pltpu.VMEM((6, 16, both), BF16),
        dma((8,)),
        dma((8,)),
    ]
    ext_shape = (3, EXT, both)
    before, active, ext = call(
        conv_kernel,
        (sds((T, both), F32), sds((T, both), BF16), sds(ext_shape, F32)),
        halo,
        0,
        (joined, taps),
    )
    raw = step_raw[0]
    flat = (width, T)
    chunks = 2 * heads
    block = pltpu.VMEM((chunks, width // heads, T), F32)
    mixed, grad_before, grad_step, params = call(
        state_kernel,
        (sds((T, width), BF16), sds((T, both), BF16), sds((T, heads), F32), sds((16, both), F32)),
        [
            block, block, block, block, block, block,
            pltpu.VMEM((chunks, T), F32),
            pltpu.VMEM((chunks, T), F32),
            pltpu.VMEM((3, heads, T), F32),
            pltpu.VMEM((tp_n, T, both - width), F32),
            dma((chunks,)), dma((chunks,)), dma((chunks,)), dma((chunks,)),
            dma((tp_n - 1,)), dma((tp_n - 1,)),
        ],
        1,
        (
            active, before, ext, cotangent[0], raw, raw.T, step_bias[None], step_bias[:, None],
            decay_log, decay_log.T, jnp.repeat(skip_gain, width // heads)[None],
            state_east.reshape(flat), state_west.reshape(flat),
        ),
    )
    totals = lax.psum(params, ("lon", "lat"))
    grad_f, grad_p = call(
        adjoint_kernel,
        (sds((T, width), BF16), sds((T, both - width), BF16)),
        [pltpu.VMEM(ext_shape, F32)] + halo,
        2,
        (grad_before, taps),
    )
    cells = T * lax.axis_size("lat") * lax.axis_size("lon")
    totals = totals * cells ** (-0.5)
    return (
        mixed[None], grad_f[None], grad_p[None], grad_step[None],
        totals[0:9, :width], totals[0:9, width:], totals[9:11, :heads],
        totals[11, :heads], totals[12, :heads],
    )


def solution(mesh):
    in_specs = (
        P("lat", "lon", "tp"),
        P("lat", "lon", None),
        P("lat", "lon", "tp"),
        P("tp"),
        P(None, "tp"),
        P("tp"),
        P(None, "tp"),
        P(),
        P("lat", "tp", None, None),
        P("lat", "tp", None, None),
        P("lat", "lon", "tp"),
    )
    out_specs = (
        P("lat", "lon", "tp"),
        P("lat", "lon", "tp"),
        P("lat", "lon", None),
        P("lat", "lon", "tp"),
        P(None, "tp"),
        P(),
        P(None, "tp"),
        P("tp"),
        P("tp"),
    )
    return jax.shard_map(shards, mesh=mesh, in_specs=in_specs, out_specs=out_specs, check_vma=False)
```

```python
from functools import partial

import jax
import jax.numpy as jnp
from jax import lax
from jax.experimental import pallas as pl
from jax.experimental.pallas import tpu as pltpu
from jax.sharding import PartitionSpec as P

MESH = pl.DeviceIdType.MESH
F32 = jnp.float32
BF16 = jnp.bfloat16
T = 128
EXT = T + 16
EDGES = ((0, -1), (0, 1), (-1, -1), (-1, 1), (1, -1), (1, 1))


def hi(a, b):
    return jnp.dot(a, b, precision=lax.Precision.HIGHEST, preferred_element_type=F32)


def nn(a, b):
    return jnp.dot(a, b, preferred_element_type=F32)


def nt(a, b):
    return lax.dot_general(a, b, (((1,), (1,)), ((), ())), preferred_element_type=F32)


def tn(a, b):
    return lax.dot_general(a, b, (((0,), (0,)), ((), ())), preferred_element_type=F32)


def grid_peer(d_lat, d_lon):
    lat_n, lon_n = lax.axis_size("lat"), lax.axis_size("lon")
    return {
        "lat": lax.rem(lax.axis_index("lat") + d_lat + lat_n, lat_n),
        "lon": lax.rem(lax.axis_index("lon") + d_lon + lon_n, lon_n),
    }


def greet(peers):
    barrier = pltpu.get_barrier_semaphore()
    for peer in peers:
        pl.semaphore_signal(barrier, inc=1, device_id=peer, device_id_type=MESH)
    pl.semaphore_wait(barrier, len(peers))


def grid_peers():
    return [grid_peer(a, b) for a in (-1, 0, 1) for b in (-1, 0, 1) if (a, b) != (0, 0)]


def halo_copies(src, lanes, rows, edges, send, recv, base):
    copies = []
    for slot, a in enumerate((-1, 1)):
        copies.append(
            pltpu.make_async_remote_copy(
                src, rows.at[slot, :, lanes], send.at[base + slot], recv.at[base + slot],
                device_id=grid_peer(-a, 0), device_id_type=MESH,
            )
        )
    for slot, (a, b) in enumerate(EDGES):
        part = src.at[pl.ds(T - 16, 16)] if b < 0 else src.at[pl.ds(0, 16)]
        copies.append(
            pltpu.make_async_remote_copy(
                part, edges.at[slot, :, lanes], send.at[base + 2 + slot], recv.at[base + 2 + slot],
                device_id=grid_peer(-a, -b), device_id_type=MESH,
            )
        )
    return copies


def fill_extended(own, lanes, rows, edges, ext):
    lat, lon = lax.axis_index("lat"), lax.axis_index("lon")
    lat_n, lon_n = lax.axis_size("lat"), lax.axis_size("lon")
    keep = {
        (1, -1): (lat > 0).astype(F32),
        (1, 1): (lat < lat_n - 1).astype(F32),
        (2, -1): (lon > 0).astype(F32),
        (2, 1): (lon < lon_n - 1).astype(F32),
    }
    ext[1, 8 : 8 + T, lanes] = own.astype(F32)
    ext[0, 8 : 8 + T, lanes] = rows[0, :, lanes].astype(F32) * keep[1, -1]
    ext[2, 8 : 8 + T, lanes] = rows[1, :, lanes].astype(F32) * keep[1, 1]
    for slot, (a, b) in enumerate(EDGES):
        scale = keep[2, b] if a == 0 else keep[2, b] * keep[1, a]
        tile = edges[slot, :, lanes].astype(F32) * scale
        if b < 0:
            ext[a + 1, 0:8, lanes] = tile[8:16]
        else:
            ext[a + 1, 8 + T :, lanes] = tile[0:8]


def stencil(ext, taps, lanes, adjoint):
    sums = []
    for b in range(3):
        total = None
        for a in range(3):
            term = taps[3 * a + b : 3 * a + b + 1, lanes] * ext[2 - a if adjoint else a, :, lanes]
            total = term if total is None else total + term
        sums.append(total)
    west, east = (sums[2], sums[0]) if adjoint else (sums[0], sums[2])
    full = pltpu.roll(west, 1, 0) + sums[1] + pltpu.roll(east, EXT - 1, 0)
    return full[8 : 8 + T]


def layer_kernel(
    features, projections, cot, raw_r, bias_r, logs_r, gain_r, taps_f, taps_p, start_e, start_w,
    mixed, out_f, out_p, grad_step, out_taps_f, out_taps_p, out_logs, out_bias, out_gain,
    before, active, ext, ext_g, grad_before, taps, rows, edges, rows_g, edges_g,
    add_r, add_l, in_r, in_l, out_r, out_l, dec_r, dec_l, cols, gathered,
    params, by_lat, by_lon, whole,
    send_h, recv_h, send_g, recv_g, send_r, recv_r, send_l, recv_l, send_t, recv_t,
    send_a, recv_a, send_b, recv_b, send_c, recv_c,
):
    lon, tp, lat = lax.axis_index("lon"), lax.axis_index("tp"), lax.axis_index("lat")
    lon_n, tp_n, lat_n = lax.axis_size("lon"), lax.axis_size("tp"), lax.axis_size("lat")
    heads = raw_r.shape[0]
    width = cot.shape[1]
    both = width + projections.shape[1]
    size = width // heads
    chunks = 2 * heads
    tp_peers = [{"tp": lax.rem(tp + d, tp_n)} for d in range(1, tp_n)]
    lat_others = [lax.rem(lat + d, lat_n) for d in range(1, lat_n)]
    lon_others = [lax.rem(lon + d, lon_n) for d in range(1, lon_n)]
    greet(
        grid_peers() + tp_peers + [{"lat": o} for o in lat_others] + [{"lon": o} for o in lon_others]
    )
    lanes_f, lanes_p = pl.ds(0, width), pl.ds(width, both - width)
    halo = halo_copies(features, lanes_f, rows, edges, send_h, recv_h, 0)
    halo += halo_copies(projections, lanes_p, rows, edges, send_h, recv_h, 8)
    for copy in halo:
        copy.start()
    taps[:, 0:width] = taps_f[...]
    taps[:, width:both] = taps_p[...]

    row_i = lax.broadcasted_iota(jnp.int32, (T, T), 0)
    col_i = lax.broadcasted_iota(jnp.int32, (T, T), 1)
    lower = (row_i >= col_i).astype(F32)
    upper = (row_i <= col_i).astype(F32)
    spread = (
        lax.broadcasted_iota(jnp.int32, (heads, width), 1) // size
        == lax.broadcasted_iota(jnp.int32, (heads, width), 0)
    ).astype(F32)
    gather = (
        lax.broadcasted_iota(jnp.int32, (width, heads), 0) // size
        == lax.broadcasted_iota(jnp.int32, (width, heads), 1)
    ).astype(F32)

    def softplus(v):
        return jnp.maximum(v, 0.0) + jnp.log1p(jnp.exp(-jnp.abs(v)))

    shifted = raw_r[...].T + bias_r[...]
    steps = softplus(shifted)
    steps_r = steps.T
    rate_e, rate_w = jnp.exp(logs_r[0:1]), jnp.exp(logs_r[1:2])
    sum_e = hi(lower, -steps * rate_e)
    sum_w = hi(upper, -steps * rate_w)
    sum_er, sum_wr = sum_e.T, sum_w.T
    tot_e, tot_w = sum_e[T - 1 : T], sum_w[0:1]
    far_e, far_w = jnp.exp(tot_e - sum_e), jnp.exp(tot_w - sum_w)
    fac_e, fac_w = far_e * steps, far_w * steps
    wide_ee, wide_ew = hi(jnp.exp(sum_e), spread), hi(jnp.exp(sum_w), spread)
    wide_fe, wide_fw = hi(fac_e, spread), hi(fac_w, spread)
    close_e = jnp.broadcast_to(jnp.exp(sum_er[:, T - 1 : T]), (heads, T))
    close_w = jnp.broadcast_to(jnp.exp(sum_wr[:, 0:1]), (heads, T))
    dec_r[0:heads] = close_e
    dec_r[heads:chunks] = close_w
    dec_l[0:heads] = close_w
    dec_l[heads:chunks] = close_e

    gain = hi(jnp.broadcast_to(gain_r[...], (8, heads)), spread)[0:1]

    for copy in halo:
        copy.wait()
    for part in range(both // 128):
        lanes = slice(128 * part, 128 * part + 128)
        if 128 * part < width:
            own = features[:, lanes]
        else:
            own = projections[:, 128 * part - width : 128 * part - width + 128]
        fill_extended(own, lanes, rows, edges, ext)
        value = stencil(ext, taps, lanes, False)
        before[:, lanes] = value
        active[:, lanes] = (value * jax.nn.sigmoid(value)).astype(BF16)

    inner = active[:, 0:width].astype(F32)
    b_part = active[:, width : width + T]
    c_part = active[:, width + T : width + 2 * T]
    incoming = cot[...].astype(F32)
    src_e, src_w = (inner * wide_fe).astype(BF16), (inner * wide_fw).astype(BF16)
    inc_e, inc_w = (incoming * wide_ee).astype(BF16), (incoming * wide_ew).astype(BF16)
    shape3 = (heads, size, T)
    add_r[0:heads] = tn(src_e, b_part).reshape(shape3)
    add_r[heads:chunks] = tn(inc_w, c_part).reshape(shape3)
    add_l[0:heads] = tn(src_w, b_part).reshape(shape3)
    add_l[heads:chunks] = tn(inc_e, c_part).reshape(shape3)

    @pl.when(lon == 0)
    def _():
        in_r[0:heads] = start_e[...].reshape(shape3)
        in_r[heads:chunks] = jnp.zeros(shape3, F32)

    @pl.when(lon == lon_n - 1)
    def _():
        in_l[0:heads] = start_w[...].reshape(shape3)
        in_l[heads:chunks] = jnp.zeros(shape3, F32)

    def copy_r(q):
        return pltpu.make_async_remote_copy(
            out_r.at[q], in_r.at[q], send_r.at[q], recv_r.at[q],
            device_id=grid_peer(0, 1), device_id_type=MESH,
        )

    def copy_l(q):
        return pltpu.make_async_remote_copy(
            out_l.at[q], in_l.at[q], send_l.at[q], recv_l.at[q],
            device_id=grid_peer(0, -1), device_id_type=MESH,
        )

    lead = 3
    skew_r = jnp.maximum(0, (2 * lon - (lon_n - 1)) * lead)
    skew_l = jnp.maximum(0, ((lon_n - 1) - 2 * lon) * lead)

    def hop(slot, _):
        q_r, q_l = slot - skew_r, slot - skew_l

        @pl.when((q_r >= 0) & (q_r < chunks))
        def _():
            @pl.when(lon > 0)
            def _():
                copy_r(q_r).wait_recv()

            @pl.when(lon < lon_n - 1)
            def _():
                out_r[q_r] = dec_r[pl.ds(q_r, 1), :] * in_r[q_r] + add_r[q_r]
                copy_r(q_r).start()

        @pl.when((q_l >= 0) & (q_l < chunks))
        def _():
            @pl.when(lon < lon_n - 1)
            def _():
                copy_l(q_l).wait_recv()

            @pl.when(lon > 0)
            def _():
                out_l[q_l] = dec_l[pl.ds(q_l, 1), :] * in_l[q_l] + add_l[q_l]
                copy_l(q_l).start()

        return 0

    slots = chunks + lead * (lon_n - 1)
    idle = (skew_r >= lead * 10) | (skew_l >= lead * 10)
    turn = jnp.where(idle, chunks, slots)
    lax.fori_loop(0, turn, hop, 0)

    scores = nt(c_part, b_part)
    head_i = lax.broadcasted_iota(jnp.int32, (T, heads), 1)
    lane_half = lax.broadcasted_iota(jnp.int32, (T, T), 1) // size
    row_l = jnp.zeros((T, heads), F32)
    row_u = jnp.zeros((T, heads), F32)
    grad_scores = jnp.zeros((T, T), F32)
    per = T // size
    mixes, pulls = [], []
    for pair in range(heads // per):
        lanes = slice(T * pair, T * pair + T)
        inner_p, incoming_p = inner[:, lanes], incoming[:, lanes]
        mix, pull = None, None
        for member in range(per):
            h = per * pair + member
            mine = (lane_half == member).astype(F32)
            inner_m = (inner_p * mine).astype(BF16)
            incoming_m = (incoming_p * mine).astype(BF16)
            gap = jnp.where(
                row_i >= col_i,
                sum_e[:, h : h + 1] - sum_er[h : h + 1],
                sum_w[:, h : h + 1] - sum_wr[h : h + 1],
            )
            decay = jnp.where(row_i == col_i, 2.0, jnp.exp(gap)) * steps_r[h : h + 1]
            grad_mix = nt(incoming_m, inner_m) * decay
            grad_scores = grad_scores + grad_mix
            weight = grad_mix * scores
            below = jnp.where(row_i > col_i, weight, 0.0)
            above = jnp.where(row_i < col_i, weight, 0.0)
            row_l = jnp.where(head_i == h, jnp.sum(below, axis=1, keepdims=True), row_l)
            row_u = jnp.where(head_i == h, jnp.sum(above, axis=1, keepdims=True), row_u)
            cols[0, h : h + 1] = jnp.sum(below, axis=0, keepdims=True)
            cols[1, h : h + 1] = jnp.sum(above, axis=0, keepdims=True)
            cols[2, h : h + 1] = jnp.sum(weight, axis=0, keepdims=True)
            mixing = (decay * scores).astype(BF16)
            y, g = nn(mixing, inner_m), tn(mixing, incoming_m)
            mix = y if mix is None else mix + y
            pull = g if pull is None else pull + g
        mixes.append(mix)
        pulls.append(pull)
    grad_inner = jnp.concatenate(pulls, axis=1)
    total = jnp.concatenate(mixes, axis=1)

    lax.fori_loop(turn, slots, hop, 0)

    def settle(q, _):
        @pl.when(lon < lon_n - 1)
        def _():
            copy_r(q).wait_send()

        @pl.when(lon > 0)
        def _():
            copy_l(q).wait_send()

        return 0

    lax.fori_loop(0, chunks, settle, 0)

    flat = (width, T)
    ent_e, adj_w = in_r[0:heads].reshape(flat), in_r[heads:chunks].reshape(flat)
    ent_w, adj_e = in_l[0:heads].reshape(flat), in_l[heads:chunks].reshape(flat)
    ent_eb, ent_wb = ent_e.astype(BF16), ent_w.astype(BF16)
    adj_eb, adj_wb = adj_e.astype(BF16), adj_w.astype(BF16)

    scores_b = grad_scores.astype(BF16)
    me = pl.ds(tp, 1)
    grad_b = tn(scores_b, c_part) + nn(src_e, adj_eb) + nn(src_w, adj_wb)
    grad_c = nn(scores_b, b_part) + nn(inc_e, ent_eb) + nn(inc_w, ent_wb)
    gathered[me, :, 0:T] = grad_b[None]
    gathered[me, :, T : 2 * T] = grad_c[None]
    copies = [
        pltpu.make_async_remote_copy(
            gathered.at[tp], gathered.at[tp], send_t.at[d], recv_t.at[d],
            device_id=peer, device_id_type=MESH,
        )
        for d, peer in enumerate(tp_peers)
    ]
    for copy in copies:
        copy.start()

    read_e = nt(c_part, ent_eb) * wide_ee
    read_w = nt(c_part, ent_wb) * wide_ew
    pull_e, pull_w = nt(b_part, adj_eb), nt(b_part, adj_wb)
    mixed[...] = (total + read_e + read_w + gain * inner).astype(BF16)
    grad_inner = grad_inner + wide_fe * pull_e + wide_fw * pull_w + gain * incoming
    r_e, r_w = hi(read_e * incoming, gather), hi(read_w * incoming, gather)
    q_e, q_w = hi(pull_e * inner, gather), hi(pull_w * inner, gather)
    ones = jnp.ones((8, T), F32)

    def per_head(v):
        return lax.dot_general(
            ones, hi(spread, v), (((1,), (1,)), ((), ())),
            precision=lax.Precision.HIGHEST, preferred_element_type=F32,
        )[0:1]

    end_e, end_w = per_head(adj_e * ent_e), per_head(adj_w * ent_w)
    w_e, w_w = fac_e * q_e, fac_w * q_w
    const_e = jnp.sum(w_e, axis=0, keepdims=True) + jnp.exp(tot_e) * end_e
    const_w = jnp.sum(w_w, axis=0, keepdims=True) + jnp.exp(tot_w) * end_w
    grad_log_e = hi(upper, row_l - cols[0].T + r_e - w_e) + const_e
    grad_log_w = hi(lower, row_u - cols[1].T + r_w - w_w) + const_w
    grad_steps = (
        (cols[2] / steps_r).T + far_e * q_e + far_w * q_w - rate_e * grad_log_e - rate_w * grad_log_w
    )
    grad_raw = grad_steps * jax.nn.sigmoid(shifted)
    grad_step[...] = grad_raw.T
    small = both // 128
    params[small:8] = jnp.zeros((8 - small, 16, 128), F32)
    params[0:small, 9:16] = jnp.zeros((small, 7, 128), F32)
    params[small, 0:1, 0:heads] = jnp.sum(-steps * rate_e * grad_log_e, axis=0, keepdims=True)
    params[small, 1:2, 0:heads] = jnp.sum(-steps * rate_w * grad_log_w, axis=0, keepdims=True)
    params[small, 2:3, 0:heads] = jnp.sum(grad_raw, axis=0, keepdims=True)
    params[small, 3:4, 0:heads] = jnp.sum(hi(incoming * inner, gather), axis=0, keepdims=True)

    def back(part, grad_active):
        lanes = slice(128 * part, 128 * part + 128)
        value = before[:, lanes]
        slope = jax.nn.sigmoid(value)
        grad = (
            grad_active.astype(BF16).astype(F32) * slope * (1.0 + value * (1.0 - slope))
        ).astype(BF16)
        grad_before[:, lanes] = grad

    def weigh(part):
        lanes = slice(128 * part, 128 * part + 128)
        edge = jnp.zeros((8, 128), F32)
        wide = jnp.concatenate([edge, grad_before[:, lanes].astype(F32), edge], axis=0)
        for b in range(3):
            moved = wide if b == 1 else pltpu.roll(wide, EXT - 1 if b == 0 else 1, 0)
            for a in range(3):
                params[part, 3 * a + b : 3 * a + b + 1] = jnp.sum(
                    moved * ext[a, :, lanes], axis=0, keepdims=True
                )

    parts_f = width // 128
    for part in range(parts_f):
        back(part, grad_inner[:, 128 * part : 128 * part + 128])
    halo_f = halo_copies(grad_before.at[:, lanes_f], lanes_f, rows_g, edges_g, send_g, recv_g, 0)
    for copy in halo_f:
        copy.start()
    for part in range(parts_f):
        weigh(part)
    for copy in copies:
        copy.wait()
    proj = gathered[0]
    for d in range(1, tp_n):
        proj = proj + gathered[d]
    for part in range(2):
        back(parts_f + part, proj[:, 128 * part : 128 * part + 128])
    halo_p = halo_copies(grad_before.at[:, lanes_p], lanes_p, rows_g, edges_g, send_g, recv_g, 8)
    for copy in halo_p:
        copy.start()
    for part in range(2):
        weigh(parts_f + part)

    per_lat = 8 // lat_n
    mine = pl.ds(lat * per_lat, per_lat)
    share = [
        pltpu.make_async_remote_copy(
            params.at[pl.ds(other * per_lat, per_lat)], by_lat.at[lat], send_a.at[d], recv_a.at[d],
            device_id={"lat": other}, device_id_type=MESH,
        )
        for d, other in enumerate(lat_others)
    ]
    for copy in share:
        copy.start()
    by_lat[pl.ds(lat, 1)] = params[mine][None]

    def adjoint(part):
        lanes = slice(128 * part, 128 * part + 128)
        fill_extended(grad_before[:, lanes], lanes, rows_g, edges_g, ext_g)
        value = stencil(ext_g, taps, lanes, True).astype(BF16)
        if part < parts_f:
            out_f[:, lanes] = value
        else:
            out_p[:, 128 * part - width : 128 * part - width + 128] = value

    for copy in share:
        copy.wait()
    sums = by_lat[0]
    for d in range(1, lat_n):
        sums = sums + by_lat[d]
    by_lon[pl.ds(lon, 1)] = sums[None]
    share = [
        pltpu.make_async_remote_copy(
            by_lon.at[lon], by_lon.at[lon], send_b.at[d], recv_b.at[d],
            device_id={"lon": other}, device_id_type=MESH,
        )
        for d, other in enumerate(lon_others)
    ]
    for copy in share:
        copy.start()
    for copy in halo_f + halo_p:
        copy.wait()
    for part in range(both // 128):
        adjoint(part)
    for copy in share:
        copy.wait()
    sums = by_lon[0]
    for d in range(1, lon_n):
        sums = sums + by_lon[d]
    cells = T * lat_n * lon_n
    whole[pl.ds(lat, 1)] = (sums * cells ** (-0.5))[None]
    share = [
        pltpu.make_async_remote_copy(
            whole.at[lat], whole.at[lat], send_c.at[d], recv_c.at[d],
            device_id={"lat": other}, device_id_type=MESH,
        )
        for d, other in enumerate(lat_others)
    ]
    for copy in share:
        copy.start()
    for copy in share:
        copy.wait()
    for part in range(both // 128):
        tile = whole[part // per_lat, part % per_lat, 0:9, :]
        if part < parts_f:
            out_taps_f[:, 128 * part : 128 * part + 128] = tile
        else:
            out_taps_p[:, 128 * (part - parts_f) : 128 * (part - parts_f) + 128] = tile
    tile = whole[small // per_lat, small % per_lat, 0:8, :]
    out_logs[...] = tile[0:2, 0:heads]
    out_bias[...] = tile[2:3, 0:heads]
    out_gain[...] = tile[3:4, 0:heads]


def finish_kernel(*refs):
    count = len(refs) // 2
    for source, target in zip(refs[:count], refs[count:]):
        target[...] = source[...]


VM = pl.BlockSpec(memory_space=pltpu.VMEM)


def shards(
    features, projections, step_raw, step_bias, decay_log, skip_gain, conv_features,
    conv_projections, state_east, state_west, cotangent,
):
    width, heads = features.shape[2], step_raw.shape[2]
    extra = projections.shape[2]
    both = width + extra
    tp_n, lat_n, lon_n = lax.axis_size("tp"), lax.axis_size("lat"), lax.axis_size("lon")
    sds = jax.ShapeDtypeStruct
    dma = pltpu.SemaphoreType.DMA
    vm = pltpu.VMEM
    flat = (width, T)
    chunks = 2 * heads
    block = vm((chunks, width // heads, T), F32)
    outs = (
        sds((T, width), BF16), sds((T, width), BF16), sds((T, extra), BF16), sds((heads, T), F32),
        sds((9, width), F32), sds((9, extra), F32), sds((2, heads), F32), sds((1, heads), F32),
        sds((1, heads), F32),
    )
    ins = (
        features[0], projections[0], cotangent[0], step_raw[0].T, step_bias[None], decay_log,
        skip_gain[None], conv_features, conv_projections, state_east.reshape(flat),
        state_west.reshape(flat),
    )
    per_lat = 8 // lat_n
    results = pl.pallas_call(
        layer_kernel,
        out_shape=outs,
        in_specs=[VM] * len(ins),
        out_specs=(VM,) * len(outs),
        scratch_shapes=[
            vm((T, both), F32), vm((T, both), BF16), vm((3, EXT, both), F32), vm((3, EXT, both), F32),
            vm((T, both), BF16), vm((9, both), F32),
            vm((2, T, both), BF16), vm((6, 16, both), BF16),
            vm((2, T, both), BF16), vm((6, 16, both), BF16),
            block, block, block, block, block, block,
            vm((chunks, T), F32), vm((chunks, T), F32), vm((3, heads, T), F32),
            vm((tp_n, T, extra), F32),
            vm((8, 16, 128), F32), vm((lat_n, per_lat, 16, 128), F32),
            vm((lon_n, per_lat, 16, 128), F32), vm((lat_n, per_lat, 16, 128), F32),
            dma((16,)), dma((16,)), dma((16,)), dma((16,)),
            dma((chunks,)), dma((chunks,)), dma((chunks,)), dma((chunks,)),
            dma((tp_n - 1,)), dma((tp_n - 1,)), dma((lat_n - 1,)), dma((lat_n - 1,)),
            dma((lon_n - 1,)), dma((lon_n - 1,)), dma((lat_n - 1,)), dma((lat_n - 1,)),
        ],
        compiler_params=pltpu.CompilerParams(
            collective_id=0, has_side_effects=True, vmem_limit_bytes=60 << 20
        ),
    )(*ins)
    mixed, grad_f, grad_p, grad_step, taps_f, taps_p, logs, bias, gain = pl.pallas_call(
        finish_kernel,
        out_shape=outs,
        in_specs=[VM] * len(outs),
        out_specs=(VM,) * len(outs),
    )(*results)
    return (
        mixed[None], grad_f[None], grad_p[None], grad_step.T[None], taps_f, taps_p, logs,
        bias[0], gain[0],
    )


def solution(mesh):
    in_specs = (
        P("lat", "lon", "tp"),
        P("lat", "lon", None),
        P("lat", "lon", "tp"),
        P("tp"),
        P(None, "tp"),
        P("tp"),
        P(None, "tp"),
        P(),
        P("lat", "tp", None, None),
        P("lat", "tp", None, None),
        P("lat", "lon", "tp"),
    )
    out_specs = (
        P("lat", "lon", "tp"),
        P("lat", "lon", "tp"),
        P("lat", "lon", None),
        P("lat", "lon", "tp"),
        P(None, "tp"),
        P(),
        P(None, "tp"),
        P("tp"),
        P("tp"),
    )
    return jax.shard_map(shards, mesh=mesh, in_specs=in_specs, out_specs=out_specs, check_vma=False)
```

```python
from functools import partial

import jax
import jax.numpy as jnp
from jax import lax
from jax.experimental import pallas as pl
from jax.experimental.pallas import tpu as pltpu
from jax.sharding import PartitionSpec as P

MESH = pl.DeviceIdType.MESH
F32 = jnp.float32
BF16 = jnp.bfloat16
T = 128
EXT = T + 16
CUT = 2
EDGES = ((0, -1), (0, 1), (-1, -1), (-1, 1), (1, -1), (1, 1))


def hi(a, b):
    return jnp.dot(a, b, precision=lax.Precision.HIGHEST, preferred_element_type=F32)


def nn(a, b):
    return jnp.dot(a, b, preferred_element_type=F32)


def nt(a, b):
    return lax.dot_general(a, b, (((1,), (1,)), ((), ())), preferred_element_type=F32)


def tn(a, b):
    return lax.dot_general(a, b, (((0,), (0,)), ((), ())), preferred_element_type=F32)


def grid_peer(d_lat, d_lon):
    lat_n, lon_n = lax.axis_size("lat"), lax.axis_size("lon")
    return {
        "lat": lax.rem(lax.axis_index("lat") + d_lat + lat_n, lat_n),
        "lon": lax.rem(lax.axis_index("lon") + d_lon + lon_n, lon_n),
    }


def greet(peers):
    barrier = pltpu.get_barrier_semaphore()
    for peer in peers:
        pl.semaphore_signal(barrier, inc=1, device_id=peer, device_id_type=MESH)
    pl.semaphore_wait(barrier, len(peers))


def grid_peers():
    return [grid_peer(a, b) for a in (-1, 0, 1) for b in (-1, 0, 1) if (a, b) != (0, 0)]


def halo_copies(src, lanes, rows, edges, send, recv, base):
    copies = []
    for slot, a in enumerate((-1, 1)):
        copies.append(
            pltpu.make_async_remote_copy(
                src, rows.at[slot, :, lanes], send.at[base + slot], recv.at[base + slot],
                device_id=grid_peer(-a, 0), device_id_type=MESH,
            )
        )
    for slot, (a, b) in enumerate(EDGES):
        part = src.at[pl.ds(T - 16, 16)] if b < 0 else src.at[pl.ds(0, 16)]
        copies.append(
            pltpu.make_async_remote_copy(
                part, edges.at[slot, :, lanes], send.at[base + 2 + slot], recv.at[base + 2 + slot],
                device_id=grid_peer(-a, -b), device_id_type=MESH,
            )
        )
    return copies


def fill_extended(own, lanes, rows, edges, ext):
    lat, lon = lax.axis_index("lat"), lax.axis_index("lon")
    lat_n, lon_n = lax.axis_size("lat"), lax.axis_size("lon")
    keep = {
        (1, -1): (lat > 0).astype(F32),
        (1, 1): (lat < lat_n - 1).astype(F32),
        (2, -1): (lon > 0).astype(F32),
        (2, 1): (lon < lon_n - 1).astype(F32),
    }
    ext[1, 8 : 8 + T, lanes] = own.astype(F32)
    ext[0, 8 : 8 + T, lanes] = rows[0, :, lanes].astype(F32) * keep[1, -1]
    ext[2, 8 : 8 + T, lanes] = rows[1, :, lanes].astype(F32) * keep[1, 1]
    for slot, (a, b) in enumerate(EDGES):
        scale = keep[2, b] if a == 0 else keep[2, b] * keep[1, a]
        tile = edges[slot, :, lanes].astype(F32) * scale
        if b < 0:
            ext[a + 1, 0:8, lanes] = tile[8:16]
        else:
            ext[a + 1, 8 + T :, lanes] = tile[0:8]


def stencil(ext, taps, lanes, adjoint):
    sums = []
    for b in range(3):
        total = None
        for a in range(3):
            term = taps[3 * a + b : 3 * a + b + 1, lanes] * ext[2 - a if adjoint else a, :, lanes]
            total = term if total is None else total + term
        sums.append(total)
    west, east = (sums[2], sums[0]) if adjoint else (sums[0], sums[2])
    full = pltpu.roll(west, 1, 0) + sums[1] + pltpu.roll(east, EXT - 1, 0)
    return full[8 : 8 + T]


def layer_kernel(
    features, projections, cot, raw_r, bias_r, logs_r, gain_r, taps_f, taps_p, start_e, start_w,
    mixed, out_f, out_p, grad_step, out_taps_f, out_taps_p, out_logs, out_bias, out_gain,
    before, active, ext, ext_g, grad_before, taps, rows, edges, rows_g, edges_g,
    add_r, add_l, in_r, in_l, out_r, out_l, dec_r, dec_l, cols, gathered,
    params, by_lat, by_lon, whole,
    send_h, recv_h, send_g, recv_g, send_r, recv_r, send_l, recv_l, send_t, recv_t,
    send_a, recv_a, send_b, recv_b, send_c, recv_c,
):
    lon, tp, lat = lax.axis_index("lon"), lax.axis_index("tp"), lax.axis_index("lat")
    lon_n, tp_n, lat_n = lax.axis_size("lon"), lax.axis_size("tp"), lax.axis_size("lat")
    heads = raw_r.shape[0]
    width = cot.shape[1]
    both = width + projections.shape[1]
    size = width // heads
    split = CUT
    chunks = 2 * heads * split
    tp_peers = [{"tp": lax.rem(tp + d, tp_n)} for d in range(1, tp_n)]
    lat_others = [lax.rem(lat + d, lat_n) for d in range(1, lat_n)]
    lon_others = [lax.rem(lon + d, lon_n) for d in range(1, lon_n)]
    greet(grid_peers() + tp_peers + [{"lat": o} for o in lat_others])
    lanes_f, lanes_p = pl.ds(0, width), pl.ds(width, both - width)
    halo = halo_copies(features, lanes_f, rows, edges, send_h, recv_h, 0)
    halo += halo_copies(projections, lanes_p, rows, edges, send_h, recv_h, 8)
    for copy in halo:
        copy.start()
    taps[:, 0:width] = taps_f[...]
    taps[:, width:both] = taps_p[...]

    row_i = lax.broadcasted_iota(jnp.int32, (T, T), 0)
    col_i = lax.broadcasted_iota(jnp.int32, (T, T), 1)
    lower = (row_i >= col_i).astype(F32)
    upper = (row_i <= col_i).astype(F32)
    spread = (
        lax.broadcasted_iota(jnp.int32, (heads, width), 1) // size
        == lax.broadcasted_iota(jnp.int32, (heads, width), 0)
    ).astype(F32)
    gather = (
        lax.broadcasted_iota(jnp.int32, (width, heads), 0) // size
        == lax.broadcasted_iota(jnp.int32, (width, heads), 1)
    ).astype(F32)

    def softplus(v):
        return jnp.maximum(v, 0.0) + jnp.log1p(jnp.exp(-jnp.abs(v)))

    shifted = raw_r[...].T + bias_r[...]
    steps = softplus(shifted)
    steps_r = steps.T
    rate_e, rate_w = jnp.exp(logs_r[0:1]), jnp.exp(logs_r[1:2])
    sum_e = hi(lower, -steps * rate_e)
    sum_w = hi(upper, -steps * rate_w)
    sum_er, sum_wr = sum_e.T, sum_w.T
    tot_e, tot_w = sum_e[T - 1 : T], sum_w[0:1]
    far_e, far_w = jnp.exp(tot_e - sum_e), jnp.exp(tot_w - sum_w)
    fac_e, fac_w = far_e * steps, far_w * steps
    wide_ee, wide_ew = hi(jnp.exp(sum_e), spread), hi(jnp.exp(sum_w), spread)
    wide_fe, wide_fw = hi(fac_e, spread), hi(fac_w, spread)
    half = heads * split
    close_e = jnp.broadcast_to(jnp.exp(sum_er[:, T - 1 : T]), (heads, T))
    close_w = jnp.broadcast_to(jnp.exp(sum_wr[:, 0:1]), (heads, T))
    for h in range(heads):
        east = jnp.broadcast_to(close_e[h : h + 1], (split, T))
        west = jnp.broadcast_to(close_w[h : h + 1], (split, T))
        dec_r[h * split : (h + 1) * split] = east
        dec_l[h * split : (h + 1) * split] = west
        dec_r[half + h * split : half + (h + 1) * split] = west
        dec_l[half + h * split : half + (h + 1) * split] = east

    gain = hi(jnp.broadcast_to(gain_r[...], (8, heads)), spread)[0:1]

    for copy in halo:
        copy.wait()
    for part in range(both // 128):
        lanes = slice(128 * part, 128 * part + 128)
        if 128 * part < width:
            own = features[:, lanes]
        else:
            own = projections[:, 128 * part - width : 128 * part - width + 128]
        fill_extended(own, lanes, rows, edges, ext)
        value = stencil(ext, taps, lanes, False)
        before[:, lanes] = value
        active[:, lanes] = (value * jax.nn.sigmoid(value)).astype(BF16)

    inner = active[:, 0:width].astype(F32)
    b_part = active[:, width : width + T]
    c_part = active[:, width + T : width + 2 * T]
    incoming = cot[...].astype(F32)
    src_e, src_w = (inner * wide_fe).astype(BF16), (inner * wide_fw).astype(BF16)
    inc_e, inc_w = (incoming * wide_ee).astype(BF16), (incoming * wide_ew).astype(BF16)
    shape3 = (half, size // split, T)
    add_r[0:half] = tn(src_e, b_part).reshape(shape3)
    add_r[half:chunks] = tn(inc_w, c_part).reshape(shape3)
    add_l[0:half] = tn(src_w, b_part).reshape(shape3)
    add_l[half:chunks] = tn(inc_e, c_part).reshape(shape3)

    @pl.when(lon == 0)
    def _():
        in_r[0:half] = start_e[...].reshape(shape3)
        in_r[half:chunks] = jnp.zeros(shape3, F32)

    @pl.when(lon == lon_n - 1)
    def _():
        in_l[0:half] = start_w[...].reshape(shape3)
        in_l[half:chunks] = jnp.zeros(shape3, F32)

    def copy_r(q):
        return pltpu.make_async_remote_copy(
            out_r.at[q], in_r.at[q], send_r.at[q], recv_r.at[q],
            device_id=grid_peer(0, 1), device_id_type=MESH,
        )

    def copy_l(q):
        return pltpu.make_async_remote_copy(
            out_l.at[q], in_l.at[q], send_l.at[q], recv_l.at[q],
            device_id=grid_peer(0, -1), device_id_type=MESH,
        )

    lead = 6
    ahead = 2 * lon - (lon_n - 1)
    skew_r = jnp.clip(ahead * lead, 0, chunks)
    skew_l = jnp.clip(-ahead * lead, 0, chunks)

    def hop(slot, _):
        q_r, q_l = slot - skew_r, slot - skew_l

        @pl.when((q_r >= 0) & (q_r < chunks))
        def _():
            @pl.when(lon > 0)
            def _():
                copy_r(q_r).wait_recv()

            @pl.when(lon < lon_n - 1)
            def _():
                out_r[q_r] = dec_r[pl.ds(q_r, 1), :] * in_r[q_r] + add_r[q_r]
                copy_r(q_r).start()

        @pl.when((q_l >= 0) & (q_l < chunks))
        def _():
            @pl.when(lon < lon_n - 1)
            def _():
                copy_l(q_l).wait_recv()

            @pl.when(lon > 0)
            def _():
                out_l[q_l] = dec_l[pl.ds(q_l, 1), :] * in_l[q_l] + add_l[q_l]
                copy_l(q_l).start()

        return 0

    slots = 2 * chunks
    idle = jnp.abs(ahead) >= (2 * lon_n) // 3
    turn = jnp.where(idle, chunks, slots)
    lax.fori_loop(0, turn, hop, 0)

    scores = nt(c_part, b_part)
    head_i = lax.broadcasted_iota(jnp.int32, (T, heads), 1)
    lane_half = lax.broadcasted_iota(jnp.int32, (T, T), 1) // size
    row_l = jnp.zeros((T, heads), F32)
    row_u = jnp.zeros((T, heads), F32)
    grad_scores = jnp.zeros((T, T), F32)
    per = T // size
    mixes, pulls = [], []
    for pair in range(heads // per):
        lanes = slice(T * pair, T * pair + T)
        inner_p, incoming_p = inner[:, lanes], incoming[:, lanes]
        mix, pull = None, None
        for member in range(per):
            h = per * pair + member
            mine = (lane_half == member).astype(F32)
            inner_m = (inner_p * mine).astype(BF16)
            incoming_m = (incoming_p * mine).astype(BF16)
            gap = jnp.where(
                row_i >= col_i,
                sum_e[:, h : h + 1] - sum_er[h : h + 1],
                sum_w[:, h : h + 1] - sum_wr[h : h + 1],
            )
            decay = jnp.where(row_i == col_i, 2.0, jnp.exp(gap)) * steps_r[h : h + 1]
            grad_mix = nt(incoming_m, inner_m) * decay
            grad_scores = grad_scores + grad_mix
            weight = grad_mix * scores
            below = jnp.where(row_i > col_i, weight, 0.0)
            above = jnp.where(row_i < col_i, weight, 0.0)
            row_l = jnp.where(head_i == h, jnp.sum(below, axis=1, keepdims=True), row_l)
            row_u = jnp.where(head_i == h, jnp.sum(above, axis=1, keepdims=True), row_u)
            cols[0, h : h + 1] = jnp.sum(below, axis=0, keepdims=True)
            cols[1, h : h + 1] = jnp.sum(above, axis=0, keepdims=True)
            cols[2, h : h + 1] = jnp.sum(weight, axis=0, keepdims=True)
            mixing = (decay * scores).astype(BF16)
            y, g = nn(mixing, inner_m), tn(mixing, incoming_m)
            mix = y if mix is None else mix + y
            pull = g if pull is None else pull + g
        mixes.append(mix)
        pulls.append(pull)
    grad_inner = jnp.concatenate(pulls, axis=1)
    total = jnp.concatenate(mixes, axis=1)

    lax.fori_loop(turn, slots, hop, 0)

    flat = (width, T)
    ent_e, adj_w = in_r[0:half].reshape(flat), in_r[half:chunks].reshape(flat)
    ent_w, adj_e = in_l[0:half].reshape(flat), in_l[half:chunks].reshape(flat)
    ent_eb, ent_wb = ent_e.astype(BF16), ent_w.astype(BF16)
    adj_eb, adj_wb = adj_e.astype(BF16), adj_w.astype(BF16)

    scores_b = grad_scores.astype(BF16)
    me = pl.ds(tp, 1)
    scores_t = (grad_scores - scores_b.astype(F32)).astype(BF16)

    def low(value, rounded):
        return (value - rounded.astype(F32)).astype(BF16)

    grad_b = (
        tn(scores_b, c_part) + tn(scores_t, c_part)
        + nn(src_e, adj_eb) + nn(src_e, low(adj_e, adj_eb))
        + nn(src_w, adj_wb) + nn(src_w, low(adj_w, adj_wb))
    )
    grad_c = (
        nn(scores_b, b_part) + nn(scores_t, b_part)
        + nn(inc_e, ent_eb) + nn(inc_e, low(ent_e, ent_eb))
        + nn(inc_w, ent_wb) + nn(inc_w, low(ent_w, ent_wb))
    )
    gathered[me, :, 0:T] = grad_b.astype(BF16)[None]
    gathered[me, :, T : 2 * T] = grad_c.astype(BF16)[None]
    copies = [
        pltpu.make_async_remote_copy(
            gathered.at[tp], gathered.at[tp], send_t.at[d], recv_t.at[d],
            device_id=peer, device_id_type=MESH,
        )
        for d, peer in enumerate(tp_peers)
    ]
    for copy in copies:
        copy.start()

    read_e = nt(c_part, ent_eb) * wide_ee
    read_w = nt(c_part, ent_wb) * wide_ew
    pull_e, pull_w = nt(b_part, adj_eb), nt(b_part, adj_wb)
    mixed[...] = (total + read_e + read_w + gain * inner).astype(BF16)
    grad_inner = grad_inner + wide_fe * pull_e + wide_fw * pull_w + gain * incoming
    r_e, r_w = hi(read_e * incoming, gather), hi(read_w * incoming, gather)
    q_e, q_w = hi(pull_e * inner, gather), hi(pull_w * inner, gather)
    ones = jnp.ones((8, T), F32)

    def per_head(v):
        return lax.dot_general(
            ones, hi(spread, v), (((1,), (1,)), ((), ())),
            precision=lax.Precision.HIGHEST, preferred_element_type=F32,
        )[0:1]

    end_e, end_w = per_head(adj_e * ent_e), per_head(adj_w * ent_w)
    w_e, w_w = fac_e * q_e, fac_w * q_w
    const_e = jnp.sum(w_e, axis=0, keepdims=True) + jnp.exp(tot_e) * end_e
    const_w = jnp.sum(w_w, axis=0, keepdims=True) + jnp.exp(tot_w) * end_w
    grad_log_e = hi(upper, row_l - cols[0].T + r_e - w_e) + const_e
    grad_log_w = hi(lower, row_u - cols[1].T + r_w - w_w) + const_w
    grad_steps = (
        (cols[2] / steps_r).T + far_e * q_e + far_w * q_w - rate_e * grad_log_e - rate_w * grad_log_w
    )
    grad_raw = grad_steps * jax.nn.sigmoid(shifted)
    grad_step[...] = grad_raw.T
    small = both // 128
    params[small:8] = jnp.zeros((8 - small, 8, 128), F32)
    params[small + 1, 0:1, 0:heads] = jnp.sum(-steps * rate_e * grad_log_e, axis=0, keepdims=True)
    params[small + 1, 1:2, 0:heads] = jnp.sum(-steps * rate_w * grad_log_w, axis=0, keepdims=True)
    params[small + 1, 2:3, 0:heads] = jnp.sum(grad_raw, axis=0, keepdims=True)
    params[small + 1, 3:4, 0:heads] = jnp.sum(hi(incoming * inner, gather), axis=0, keepdims=True)

    def back(part, grad_active):
        lanes = slice(128 * part, 128 * part + 128)
        value = before[:, lanes]
        slope = jax.nn.sigmoid(value)
        grad = (
            grad_active.astype(BF16).astype(F32) * slope * (1.0 + value * (1.0 - slope))
        ).astype(BF16)
        grad_before[:, lanes] = grad

    def weigh(part):
        lanes = slice(128 * part, 128 * part + 128)
        edge = jnp.zeros((8, 128), F32)
        wide = jnp.concatenate([edge, grad_before[:, lanes].astype(F32), edge], axis=0)
        for b in range(3):
            moved = wide if b == 1 else pltpu.roll(wide, EXT - 1 if b == 0 else 1, 0)
            for a in range(3):
                tap = jnp.sum(moved * ext[a, :, lanes], axis=0, keepdims=True)
                if 3 * a + b < 8:
                    params[part, 3 * a + b : 3 * a + b + 1] = tap
                else:
                    params[small, part : part + 1] = tap

    parts_f = width // 128
    for part in range(parts_f):
        back(part, grad_inner[:, 128 * part : 128 * part + 128])
    halo_f = halo_copies(grad_before.at[:, lanes_f], lanes_f, rows_g, edges_g, send_g, recv_g, 0)
    for copy in halo_f:
        copy.start()
    for part in range(parts_f):
        weigh(part)
    for copy in copies:
        copy.wait()
    proj = gathered[0].astype(F32)
    for d in range(1, tp_n):
        proj = proj + gathered[d].astype(F32)
    for part in range(2):
        back(parts_f + part, proj[:, 128 * part : 128 * part + 128])
    halo_p = halo_copies(grad_before.at[:, lanes_p], lanes_p, rows_g, edges_g, send_g, recv_g, 8)
    for copy in halo_p:
        copy.start()
    for part in range(2):
        weigh(parts_f + part)

    per_lat = 8 // lat_n
    mine = pl.ds(lat * per_lat, per_lat)
    share = [
        pltpu.make_async_remote_copy(
            params.at[pl.ds(other * per_lat, per_lat)], by_lat.at[lat], send_a.at[d], recv_a.at[d],
            device_id={"lat": other}, device_id_type=MESH,
        )
        for d, other in enumerate(lat_others)
    ]
    for copy in share:
        copy.start()
    by_lat[pl.ds(lat, 1)] = params[mine][None]

    def adjoint(part):
        lanes = slice(128 * part, 128 * part + 128)
        fill_extended(grad_before[:, lanes], lanes, rows_g, edges_g, ext_g)
        value = stencil(ext_g, taps, lanes, True).astype(BF16)
        if part < parts_f:
            out_f[:, lanes] = value
        else:
            out_p[:, 128 * part - width : 128 * part - width + 128] = value

    for copy in share:
        copy.wait()
    sums = by_lat[0]
    for d in range(1, lat_n):
        sums = sums + by_lat[d]
    by_lon[pl.ds(lon, 1)] = sums[None]
    share = [
        pltpu.make_async_remote_copy(
            by_lon.at[lon], by_lon.at[lon], send_b.at[d], recv_b.at[d],
            device_id={"lon": other}, device_id_type=MESH,
        )
        for d, other in enumerate(lon_others)
    ]
    for copy in share:
        copy.start()
    for copy in halo_f + halo_p:
        copy.wait()
    for part in range(both // 128):
        adjoint(part)
    for copy in share:
        copy.wait()
    sums = by_lon[0]
    for d in range(1, lon_n):
        sums = sums + by_lon[d]
    cells = T * lat_n * lon_n
    whole[pl.ds(lat, 1)] = (sums * cells ** (-0.5))[None]
    share = [
        pltpu.make_async_remote_copy(
            whole.at[lat], whole.at[lat], send_c.at[d], recv_c.at[d],
            device_id={"lat": other}, device_id_type=MESH,
        )
        for d, other in enumerate(lat_others)
    ]
    for copy in share:
        copy.start()

    def settle(q, _):
        @pl.when(lon < lon_n - 1)
        def _():
            copy_r(q).wait_send()

        @pl.when(lon > 0)
        def _():
            copy_l(q).wait_send()

        return 0

    lax.fori_loop(0, chunks, settle, 0)

    for copy in share:
        copy.wait()
    for part in range(both // 128):
        tile = whole[part // per_lat, part % per_lat]
        last = whole[small // per_lat, small % per_lat, part : part + 1]
        target = out_taps_f if part < parts_f else out_taps_p
        lanes = slice(128 * (part % parts_f), 128 * (part % parts_f) + 128)
        target[0:8, lanes] = tile
        target[8:9, lanes] = last
    tile = whole[(small + 1) // per_lat, (small + 1) % per_lat]
    out_logs[...] = tile[0:2, 0:heads]
    out_bias[...] = tile[2:3, 0:heads]
    out_gain[...] = tile[3:4, 0:heads]


def finish_kernel(*refs):
    count = len(refs) // 2
    for source, target in zip(refs[:count], refs[count:]):
        target[...] = source[...]


VM = pl.BlockSpec(memory_space=pltpu.VMEM)


def shards(
    features, projections, step_raw, step_bias, decay_log, skip_gain, conv_features,
    conv_projections, state_east, state_west, cotangent,
):
    width, heads = features.shape[2], step_raw.shape[2]
    extra = projections.shape[2]
    both = width + extra
    tp_n, lat_n, lon_n = lax.axis_size("tp"), lax.axis_size("lat"), lax.axis_size("lon")
    sds = jax.ShapeDtypeStruct
    dma = pltpu.SemaphoreType.DMA
    vm = pltpu.VMEM
    flat = (width, T)
    chunks = 2 * heads * CUT
    block = vm((chunks, width // heads // CUT, T), F32)
    outs = (
        sds((T, width), BF16), sds((T, width), BF16), sds((T, extra), BF16), sds((heads, T), F32),
        sds((9, width), F32), sds((9, extra), F32), sds((2, heads), F32), sds((1, heads), F32),
        sds((1, heads), F32),
    )
    ins = (
        features[0], projections[0], cotangent[0], step_raw[0].T, step_bias[None], decay_log,
        skip_gain[None], conv_features, conv_projections, state_east.reshape(flat),
        state_west.reshape(flat),
    )
    per_lat = 8 // lat_n
    results = pl.pallas_call(
        layer_kernel,
        out_shape=outs,
        in_specs=[VM] * len(ins),
        out_specs=(VM,) * len(outs),
        scratch_shapes=[
            vm((T, both), F32), vm((T, both), BF16), vm((3, EXT, both), F32), vm((3, EXT, both), F32),
            vm((T, both), BF16), vm((9, both), F32),
            vm((2, T, both), BF16), vm((6, 16, both), BF16),
            vm((2, T, both), BF16), vm((6, 16, both), BF16),
            block, block, block, block, block, block,
            vm((chunks, T), F32), vm((chunks, T), F32), vm((3, heads, T), F32),
            vm((tp_n, T, extra), BF16),
            vm((8, 8, 128), F32), vm((lat_n, per_lat, 8, 128), F32),
            vm((lon_n, per_lat, 8, 128), F32), vm((lat_n, per_lat, 8, 128), F32),
            dma((16,)), dma((16,)), dma((16,)), dma((16,)),
            dma((chunks,)), dma((chunks,)), dma((chunks,)), dma((chunks,)),
            dma((tp_n - 1,)), dma((tp_n - 1,)), dma((lat_n - 1,)), dma((lat_n - 1,)),
            dma((lon_n - 1,)), dma((lon_n - 1,)), dma((lat_n - 1,)), dma((lat_n - 1,)),
        ],
        compiler_params=pltpu.CompilerParams(
            collective_id=0, has_side_effects=True, vmem_limit_bytes=60 << 20
        ),
    )(*ins)
    mixed, grad_f, grad_p, grad_step, taps_f, taps_p, logs, bias, gain = pl.pallas_call(
        finish_kernel,
        out_shape=outs,
        in_specs=[VM] * len(outs),
        out_specs=(VM,) * len(outs),
    )(*results)
    return (
        mixed[None], grad_f[None], grad_p[None], grad_step.T[None], taps_f, taps_p, logs,
        bias[0], gain[0],
    )


def solution(mesh):
    in_specs = (
        P("lat", "lon", "tp"),
        P("lat", "lon", None),
        P("lat", "lon", "tp"),
        P("tp"),
        P(None, "tp"),
        P("tp"),
        P(None, "tp"),
        P(),
        P("lat", "tp", None, None),
        P("lat", "tp", None, None),
        P("lat", "lon", "tp"),
    )
    out_specs = (
        P("lat", "lon", "tp"),
        P("lat", "lon", "tp"),
        P("lat", "lon", None),
        P("lat", "lon", "tp"),
        P(None, "tp"),
        P(),
        P(None, "tp"),
        P("tp"),
        P("tp"),
    )
    return jax.shard_map(shards, mesh=mesh, in_specs=in_specs, out_specs=out_specs, check_vma=False)
```

```python
from functools import partial

import jax
import jax.numpy as jnp
from jax import lax
from jax.experimental import pallas as pl
from jax.experimental.pallas import tpu as pltpu
from jax.sharding import PartitionSpec as P

MESH = pl.DeviceIdType.MESH
F32 = jnp.float32
BF16 = jnp.bfloat16
T = 128
EXT = T + 16
CUT = 2
EDGES = ((0, -1), (0, 1), (-1, -1), (-1, 1), (1, -1), (1, 1))


def hi(a, b):
    return jnp.dot(a, b, precision=lax.Precision.HIGHEST, preferred_element_type=F32)


def nn(a, b):
    return jnp.dot(a, b, preferred_element_type=F32)


def nt(a, b):
    return lax.dot_general(a, b, (((1,), (1,)), ((), ())), preferred_element_type=F32)


def tn(a, b):
    return lax.dot_general(a, b, (((0,), (0,)), ((), ())), preferred_element_type=F32)


def grid_peer(d_lat, d_lon):
    lat_n, lon_n = lax.axis_size("lat"), lax.axis_size("lon")
    return {
        "lat": lax.rem(lax.axis_index("lat") + d_lat + lat_n, lat_n),
        "lon": lax.rem(lax.axis_index("lon") + d_lon + lon_n, lon_n),
    }


def greet(peers):
    barrier = pltpu.get_barrier_semaphore()
    for peer in peers:
        pl.semaphore_signal(barrier, inc=1, device_id=peer, device_id_type=MESH)
    pl.semaphore_wait(barrier, len(peers))


def grid_peers():
    return [grid_peer(a, b) for a in (-1, 0, 1) for b in (-1, 0, 1) if (a, b) != (0, 0)]


def halo_copies(src, lanes, rows, edges, send, recv, base):
    copies = []
    for slot, a in enumerate((-1, 1)):
        copies.append(
            pltpu.make_async_remote_copy(
                src, rows.at[slot, :, lanes], send.at[base + slot], recv.at[base + slot],
                device_id=grid_peer(-a, 0), device_id_type=MESH,
            )
        )
    for slot, (a, b) in enumerate(EDGES):
        part = src.at[pl.ds(T - 16, 16)] if b < 0 else src.at[pl.ds(0, 16)]
        copies.append(
            pltpu.make_async_remote_copy(
                part, edges.at[slot, :, lanes], send.at[base + 2 + slot], recv.at[base + 2 + slot],
                device_id=grid_peer(-a, -b), device_id_type=MESH,
            )
        )
    return copies


def fill_extended(own, lanes, rows, edges, ext):
    lat, lon = lax.axis_index("lat"), lax.axis_index("lon")
    lat_n, lon_n = lax.axis_size("lat"), lax.axis_size("lon")
    keep = {
        (1, -1): (lat > 0).astype(F32),
        (1, 1): (lat < lat_n - 1).astype(F32),
        (2, -1): (lon > 0).astype(F32),
        (2, 1): (lon < lon_n - 1).astype(F32),
    }
    ext[1, 8 : 8 + T, lanes] = own.astype(F32)
    ext[0, 8 : 8 + T, lanes] = rows[0, :, lanes].astype(F32) * keep[1, -1]
    ext[2, 8 : 8 + T, lanes] = rows[1, :, lanes].astype(F32) * keep[1, 1]
    for slot, (a, b) in enumerate(EDGES):
        scale = keep[2, b] if a == 0 else keep[2, b] * keep[1, a]
        tile = edges[slot, :, lanes].astype(F32) * scale
        if b < 0:
            ext[a + 1, 0:8, lanes] = tile[8:16]
        else:
            ext[a + 1, 8 + T :, lanes] = tile[0:8]


def stencil(ext, taps, lanes, adjoint):
    sums = []
    for b in range(3):
        total = None
        for a in range(3):
            term = taps[3 * a + b : 3 * a + b + 1, lanes] * ext[2 - a if adjoint else a, :, lanes]
            total = term if total is None else total + term
        sums.append(total)
    west, east = (sums[2], sums[0]) if adjoint else (sums[0], sums[2])
    full = pltpu.roll(west, 1, 0) + sums[1] + pltpu.roll(east, EXT - 1, 0)
    return full[8 : 8 + T]


def layer_kernel(
    features, projections, cot, raw_r, bias_r, logs_r, gain_r, taps_f, taps_p, start_e, start_w,
    mixed, out_f, out_p, grad_step, out_taps_f, out_taps_p, out_logs, out_bias, out_gain,
    before, active, ext, ext_g, grad_before, taps, rows, edges, rows_g, edges_g,
    add_r, add_l, in_r, in_l, out_r, out_l, dec_r, dec_l, cols, gathered,
    params, by_lat, by_lon, whole,
    send_h, recv_h, send_g, recv_g, send_r, recv_r, send_l, recv_l, send_t, recv_t,
    send_a, recv_a, send_b, recv_b, send_c, recv_c,
):
    lon, tp, lat = lax.axis_index("lon"), lax.axis_index("tp"), lax.axis_index("lat")
    lon_n, tp_n, lat_n = lax.axis_size("lon"), lax.axis_size("tp"), lax.axis_size("lat")
    heads = raw_r.shape[0]
    width = cot.shape[1]
    both = width + projections.shape[1]
    size = width // heads
    split = CUT
    chunks = 2 * heads * split
    tp_peers = [{"tp": lax.rem(tp + d, tp_n)} for d in range(1, tp_n)]
    lat_others = [lax.rem(lat + d, lat_n) for d in range(1, lat_n)]
    lon_others = [lax.rem(lon + d, lon_n) for d in range(1, lon_n)]
    greet(grid_peers() + tp_peers + [{"lat": o} for o in lat_others])
    lanes_f, lanes_p = pl.ds(0, width), pl.ds(width, both - width)
    halo = halo_copies(features, lanes_f, rows, edges, send_h, recv_h, 0)
    halo += halo_copies(projections, lanes_p, rows, edges, send_h, recv_h, 8)
    for copy in halo:
        copy.start()
    taps[:, 0:width] = taps_f[...]
    taps[:, width:both] = taps_p[...]

    row_i = lax.broadcasted_iota(jnp.int32, (T, T), 0)
    col_i = lax.broadcasted_iota(jnp.int32, (T, T), 1)
    lower = (row_i >= col_i).astype(F32)
    upper = (row_i <= col_i).astype(F32)
    spread = (
        lax.broadcasted_iota(jnp.int32, (heads, width), 1) // size
        == lax.broadcasted_iota(jnp.int32, (heads, width), 0)
    ).astype(F32)
    gather = (
        lax.broadcasted_iota(jnp.int32, (width, heads), 0) // size
        == lax.broadcasted_iota(jnp.int32, (width, heads), 1)
    ).astype(F32)

    def softplus(v):
        return jnp.maximum(v, 0.0) + jnp.log1p(jnp.exp(-jnp.abs(v)))

    shifted = raw_r[...].T + bias_r[...]
    steps = softplus(shifted)
    steps_r = steps.T
    rate_e, rate_w = jnp.exp(logs_r[0:1]), jnp.exp(logs_r[1:2])
    sum_e = hi(lower, -steps * rate_e)
    sum_w = hi(upper, -steps * rate_w)
    sum_er, sum_wr = sum_e.T, sum_w.T
    tot_e, tot_w = sum_e[T - 1 : T], sum_w[0:1]
    far_e, far_w = jnp.exp(tot_e - sum_e), jnp.exp(tot_w - sum_w)
    fac_e, fac_w = far_e * steps, far_w * steps
    wide_ee, wide_ew = hi(jnp.exp(sum_e), spread), hi(jnp.exp(sum_w), spread)
    wide_fe, wide_fw = hi(fac_e, spread), hi(fac_w, spread)
    half = heads * split
    close_e = jnp.broadcast_to(jnp.exp(sum_er[:, T - 1 : T]), (heads, T))
    close_w = jnp.broadcast_to(jnp.exp(sum_wr[:, 0:1]), (heads, T))
    for h in range(heads):
        east = jnp.broadcast_to(close_e[h : h + 1], (split, T))
        west = jnp.broadcast_to(close_w[h : h + 1], (split, T))
        dec_r[h * split : (h + 1) * split] = east
        dec_l[h * split : (h + 1) * split] = west
        dec_r[half + h * split : half + (h + 1) * split] = west
        dec_l[half + h * split : half + (h + 1) * split] = east

    gain = hi(jnp.broadcast_to(gain_r[...], (8, heads)), spread)[0:1]

    for copy in halo:
        copy.wait()
    for part in range(both // 128):
        lanes = slice(128 * part, 128 * part + 128)
        if 128 * part < width:
            own = features[:, lanes]
        else:
            own = projections[:, 128 * part - width : 128 * part - width + 128]
        fill_extended(own, lanes, rows, edges, ext)
        value = stencil(ext, taps, lanes, False)
        before[:, lanes] = value
        active[:, lanes] = (value * jax.nn.sigmoid(value)).astype(BF16)

    inner = active[:, 0:width].astype(F32)
    b_part = active[:, width : width + T]
    c_part = active[:, width + T : width + 2 * T]
    incoming = cot[...].astype(F32)
    src_e, src_w = (inner * wide_fe).astype(BF16), (inner * wide_fw).astype(BF16)
    inc_e, inc_w = (incoming * wide_ee).astype(BF16), (incoming * wide_ew).astype(BF16)
    shape3 = (half, size // split, T)
    add_r[0:half] = tn(src_e, b_part).reshape(shape3)
    add_r[half:chunks] = tn(inc_w, c_part).reshape(shape3)
    add_l[0:half] = tn(src_w, b_part).reshape(shape3)
    add_l[half:chunks] = tn(inc_e, c_part).reshape(shape3)

    @pl.when(lon == 0)
    def _():
        in_r[0:half] = start_e[...].reshape(shape3)
        in_r[half:chunks] = jnp.zeros(shape3, F32)

    @pl.when(lon == lon_n - 1)
    def _():
        in_l[0:half] = start_w[...].reshape(shape3)
        in_l[half:chunks] = jnp.zeros(shape3, F32)

    def copy_r(q):
        return pltpu.make_async_remote_copy(
            out_r.at[q], in_r.at[q], send_r.at[q], recv_r.at[q],
            device_id=grid_peer(0, 1), device_id_type=MESH,
        )

    def copy_l(q):
        return pltpu.make_async_remote_copy(
            out_l.at[q], in_l.at[q], send_l.at[q], recv_l.at[q],
            device_id=grid_peer(0, -1), device_id_type=MESH,
        )

    lead = 13
    ahead = 2 * lon - (lon_n - 1)
    skew_r = jnp.clip(ahead * lead, 0, chunks)
    skew_l = jnp.clip(-ahead * lead, 0, chunks)

    def hop(slot, _):
        q_r, q_l = slot - skew_r, slot - skew_l

        @pl.when((q_r >= 0) & (q_r < chunks))
        def _():
            @pl.when(lon > 0)
            def _():
                copy_r(q_r).wait_recv()

            @pl.when(lon < lon_n - 1)
            def _():
                out_r[q_r] = dec_r[pl.ds(q_r, 1), :] * in_r[q_r] + add_r[q_r]
                copy_r(q_r).start()

        @pl.when((q_l >= 0) & (q_l < chunks))
        def _():
            @pl.when(lon < lon_n - 1)
            def _():
                copy_l(q_l).wait_recv()

            @pl.when(lon > 0)
            def _():
                out_l[q_l] = dec_l[pl.ds(q_l, 1), :] * in_l[q_l] + add_l[q_l]
                copy_l(q_l).start()

        return 0

    slots = 2 * chunks
    idle = jnp.abs(ahead) >= (2 * lon_n) // 3
    turn = jnp.where(idle, chunks, slots)
    lax.fori_loop(0, turn, hop, 0)

    scores = nt(c_part, b_part)
    head_i = lax.broadcasted_iota(jnp.int32, (T, heads), 1)
    lane_half = lax.broadcasted_iota(jnp.int32, (T, T), 1) // size
    row_l = jnp.zeros((T, heads), F32)
    row_u = jnp.zeros((T, heads), F32)
    grad_scores = jnp.zeros((T, T), F32)
    per = T // size
    mixes, pulls = [], []
    for pair in range(heads // per):
        lanes = slice(T * pair, T * pair + T)
        inner_p, incoming_p = inner[:, lanes], incoming[:, lanes]
        mix, pull = None, None
        for member in range(per):
            h = per * pair + member
            mine = (lane_half == member).astype(F32)
            inner_m = (inner_p * mine).astype(BF16)
            incoming_m = (incoming_p * mine).astype(BF16)
            gap = jnp.where(
                row_i >= col_i,
                sum_e[:, h : h + 1] - sum_er[h : h + 1],
                sum_w[:, h : h + 1] - sum_wr[h : h + 1],
            )
            decay = jnp.where(row_i == col_i, 2.0, jnp.exp(gap)) * steps_r[h : h + 1]
            grad_mix = nt(incoming_m, inner_m) * decay
            grad_scores = grad_scores + grad_mix
            weight = grad_mix * scores
            below = jnp.where(row_i > col_i, weight, 0.0)
            above = jnp.where(row_i < col_i, weight, 0.0)
            row_l = jnp.where(head_i == h, jnp.sum(below, axis=1, keepdims=True), row_l)
            row_u = jnp.where(head_i == h, jnp.sum(above, axis=1, keepdims=True), row_u)
            cols[0, h : h + 1] = jnp.sum(below, axis=0, keepdims=True)
            cols[1, h : h + 1] = jnp.sum(above, axis=0, keepdims=True)
            cols[2, h : h + 1] = jnp.sum(weight, axis=0, keepdims=True)
            mixing = (decay * scores).astype(BF16)
            y, g = nn(mixing, inner_m), tn(mixing, incoming_m)
            mix = y if mix is None else mix + y
            pull = g if pull is None else pull + g
        mixes.append(mix)
        pulls.append(pull)
    grad_inner = jnp.concatenate(pulls, axis=1)
    total = jnp.concatenate(mixes, axis=1)

    lax.fori_loop(turn, slots, hop, 0)

    flat = (width, T)
    ent_e, adj_w = in_r[0:half].reshape(flat), in_r[half:chunks].reshape(flat)
    ent_w, adj_e = in_l[0:half].reshape(flat), in_l[half:chunks].reshape(flat)
    ent_eb, ent_wb = ent_e.astype(BF16), ent_w.astype(BF16)
    adj_eb, adj_wb = adj_e.astype(BF16), adj_w.astype(BF16)

    scores_b = grad_scores.astype(BF16)
    me = pl.ds(tp, 1)
    scores_t = (grad_scores - scores_b.astype(F32)).astype(BF16)

    def low(value, rounded):
        return (value - rounded.astype(F32)).astype(BF16)

    grad_b = (
        tn(scores_b, c_part) + tn(scores_t, c_part)
        + nn(src_e, adj_eb) + nn(src_e, low(adj_e, adj_eb))
        + nn(src_w, adj_wb) + nn(src_w, low(adj_w, adj_wb))
    )
    grad_c = (
        nn(scores_b, b_part) + nn(scores_t, b_part)
        + nn(inc_e, ent_eb) + nn(inc_e, low(ent_e, ent_eb))
        + nn(inc_w, ent_wb) + nn(inc_w, low(ent_w, ent_wb))
    )
    gathered[me, :, 0:T] = grad_b.astype(BF16)[None]
    gathered[me, :, T : 2 * T] = grad_c.astype(BF16)[None]
    copies = [
        pltpu.make_async_remote_copy(
            gathered.at[tp], gathered.at[tp], send_t.at[d], recv_t.at[d],
            device_id=peer, device_id_type=MESH,
        )
        for d, peer in enumerate(tp_peers)
    ]
    for copy in copies:
        copy.start()

    read_e = nt(c_part, ent_eb) * wide_ee
    read_w = nt(c_part, ent_wb) * wide_ew
    pull_e, pull_w = nt(b_part, adj_eb), nt(b_part, adj_wb)
    mixed[...] = (total + read_e + read_w + gain * inner).astype(BF16)
    grad_inner = grad_inner + wide_fe * pull_e + wide_fw * pull_w + gain * incoming
    r_e, r_w = hi(read_e * incoming, gather), hi(read_w * incoming, gather)
    q_e, q_w = hi(pull_e * inner, gather), hi(pull_w * inner, gather)
    ones = jnp.ones((8, T), F32)

    def per_head(v):
        return lax.dot_general(
            ones, hi(spread, v), (((1,), (1,)), ((), ())),
            precision=lax.Precision.HIGHEST, preferred_element_type=F32,
        )[0:1]

    end_e, end_w = per_head(adj_e * ent_e), per_head(adj_w * ent_w)
    w_e, w_w = fac_e * q_e, fac_w * q_w
    const_e = jnp.sum(w_e, axis=0, keepdims=True) + jnp.exp(tot_e) * end_e
    const_w = jnp.sum(w_w, axis=0, keepdims=True) + jnp.exp(tot_w) * end_w
    grad_log_e = hi(upper, row_l - cols[0].T + r_e - w_e) + const_e
    grad_log_w = hi(lower, row_u - cols[1].T + r_w - w_w) + const_w
    grad_steps = (
        (cols[2] / steps_r).T + far_e * q_e + far_w * q_w - rate_e * grad_log_e - rate_w * grad_log_w
    )
    grad_raw = grad_steps * jax.nn.sigmoid(shifted)
    grad_step[...] = grad_raw.T
    small = both // 128
    params[small:8] = jnp.zeros((8 - small, 8, 128), F32)
    params[small + 1, 0:1, 0:heads] = jnp.sum(-steps * rate_e * grad_log_e, axis=0, keepdims=True)
    params[small + 1, 1:2, 0:heads] = jnp.sum(-steps * rate_w * grad_log_w, axis=0, keepdims=True)
    params[small + 1, 2:3, 0:heads] = jnp.sum(grad_raw, axis=0, keepdims=True)
    params[small + 1, 3:4, 0:heads] = jnp.sum(hi(incoming * inner, gather), axis=0, keepdims=True)

    def back(part, grad_active):
        lanes = slice(128 * part, 128 * part + 128)
        value = before[:, lanes]
        slope = jax.nn.sigmoid(value)
        grad = (
            grad_active.astype(BF16).astype(F32) * slope * (1.0 + value * (1.0 - slope))
        ).astype(BF16)
        grad_before[:, lanes] = grad

    def weigh(part):
        lanes = slice(128 * part, 128 * part + 128)
        edge = jnp.zeros((8, 128), F32)
        wide = jnp.concatenate([edge, grad_before[:, lanes].astype(F32), edge], axis=0)
        for b in range(3):
            moved = wide if b == 1 else pltpu.roll(wide, EXT - 1 if b == 0 else 1, 0)
            for a in range(3):
                tap = jnp.sum(moved * ext[a, :, lanes], axis=0, keepdims=True)
                if 3 * a + b < 8:
                    params[part, 3 * a + b : 3 * a + b + 1] = tap
                else:
                    params[small, part : part + 1] = tap

    parts_f = width // 128
    for part in range(parts_f):
        back(part, grad_inner[:, 128 * part : 128 * part + 128])
    halo_f = halo_copies(grad_before.at[:, lanes_f], lanes_f, rows_g, edges_g, send_g, recv_g, 0)
    for copy in halo_f:
        copy.start()
    for part in range(parts_f):
        weigh(part)
    for copy in copies:
        copy.wait()
    proj = gathered[0].astype(F32)
    for d in range(1, tp_n):
        proj = proj + gathered[d].astype(F32)
    for part in range(2):
        back(parts_f + part, proj[:, 128 * part : 128 * part + 128])
    halo_p = halo_copies(grad_before.at[:, lanes_p], lanes_p, rows_g, edges_g, send_g, recv_g, 8)
    for copy in halo_p:
        copy.start()
    for part in range(2):
        weigh(parts_f + part)

    per_lat = 8 // lat_n
    mine = pl.ds(lat * per_lat, per_lat)
    share = [
        pltpu.make_async_remote_copy(
            params.at[pl.ds(other * per_lat, per_lat)], by_lat.at[lat], send_a.at[d], recv_a.at[d],
            device_id={"lat": other}, device_id_type=MESH,
        )
        for d, other in enumerate(lat_others)
    ]
    for copy in share:
        copy.start()
    by_lat[pl.ds(lat, 1)] = params[mine][None]

    def adjoint(part):
        lanes = slice(128 * part, 128 * part + 128)
        fill_extended(grad_before[:, lanes], lanes, rows_g, edges_g, ext_g)
        value = stencil(ext_g, taps, lanes, True).astype(BF16)
        if part < parts_f:
            out_f[:, lanes] = value
        else:
            out_p[:, 128 * part - width : 128 * part - width + 128] = value

    for copy in share:
        copy.wait()
    sums = by_lat[0]
    for d in range(1, lat_n):
        sums = sums + by_lat[d]
    by_lon[pl.ds(lon, 1)] = sums[None]
    share = [
        pltpu.make_async_remote_copy(
            by_lon.at[lon], by_lon.at[lon], send_b.at[d], recv_b.at[d],
            device_id={"lon": other}, device_id_type=MESH,
        )
        for d, other in enumerate(lon_others)
    ]
    for copy in share:
        copy.start()
    for copy in halo_f + halo_p:
        copy.wait()
    for part in range(both // 128):
        adjoint(part)
    for copy in share:
        copy.wait()
    sums = by_lon[0]
    for d in range(1, lon_n):
        sums = sums + by_lon[d]
    cells = T * lat_n * lon_n
    whole[pl.ds(lat, 1)] = (sums * cells ** (-0.5))[None]
    share = [
        pltpu.make_async_remote_copy(
            whole.at[lat], whole.at[lat], send_c.at[d], recv_c.at[d],
            device_id={"lat": other}, device_id_type=MESH,
        )
        for d, other in enumerate(lat_others)
    ]
    for copy in share:
        copy.start()

    def settle(q, _):
        @pl.when(lon < lon_n - 1)
        def _():
            copy_r(q).wait_send()

        @pl.when(lon > 0)
        def _():
            copy_l(q).wait_send()

        return 0

    lax.fori_loop(0, chunks, settle, 0)

    for copy in share:
        copy.wait()
    for part in range(both // 128):
        tile = whole[part // per_lat, part % per_lat]
        last = whole[small // per_lat, small % per_lat, part : part + 1]
        target = out_taps_f if part < parts_f else out_taps_p
        lanes = slice(128 * (part % parts_f), 128 * (part % parts_f) + 128)
        target[0:8, lanes] = tile
        target[8:9, lanes] = last
    tile = whole[(small + 1) // per_lat, (small + 1) % per_lat]
    out_logs[...] = tile[0:2, 0:heads]
    out_bias[...] = tile[2:3, 0:heads]
    out_gain[...] = tile[3:4, 0:heads]


def finish_kernel(*refs):
    count = len(refs) // 2
    for source, target in zip(refs[:count], refs[count:]):
        target[...] = source[...]


VM = pl.BlockSpec(memory_space=pltpu.VMEM)


def shards(
    features, projections, step_raw, step_bias, decay_log, skip_gain, conv_features,
    conv_projections, state_east, state_west, cotangent,
):
    width, heads = features.shape[2], step_raw.shape[2]
    extra = projections.shape[2]
    both = width + extra
    tp_n, lat_n, lon_n = lax.axis_size("tp"), lax.axis_size("lat"), lax.axis_size("lon")
    sds = jax.ShapeDtypeStruct
    dma = pltpu.SemaphoreType.DMA
    vm = pltpu.VMEM
    flat = (width, T)
    chunks = 2 * heads * CUT
    block = vm((chunks, width // heads // CUT, T), F32)
    outs = (
        sds((T, width), BF16), sds((T, width), BF16), sds((T, extra), BF16), sds((heads, T), F32),
        sds((9, width), F32), sds((9, extra), F32), sds((2, heads), F32), sds((1, heads), F32),
        sds((1, heads), F32),
    )
    ins = (
        features[0], projections[0], cotangent[0], step_raw[0].T, step_bias[None], decay_log,
        skip_gain[None], conv_features, conv_projections, state_east.reshape(flat),
        state_west.reshape(flat),
    )
    per_lat = 8 // lat_n
    results = pl.pallas_call(
        layer_kernel,
        out_shape=outs,
        in_specs=[VM] * len(ins),
        out_specs=(VM,) * len(outs),
        scratch_shapes=[
            vm((T, both), F32), vm((T, both), BF16), vm((3, EXT, both), F32), vm((3, EXT, both), F32),
            vm((T, both), BF16), vm((9, both), F32),
            vm((2, T, both), BF16), vm((6, 16, both), BF16),
            vm((2, T, both), BF16), vm((6, 16, both), BF16),
            block, block, block, block, block, block,
            vm((chunks, T), F32), vm((chunks, T), F32), vm((3, heads, T), F32),
            vm((tp_n, T, extra), BF16),
            vm((8, 8, 128), F32), vm((lat_n, per_lat, 8, 128), F32),
            vm((lon_n, per_lat, 8, 128), F32), vm((lat_n, per_lat, 8, 128), F32),
            dma((16,)), dma((16,)), dma((16,)), dma((16,)),
            dma((chunks,)), dma((chunks,)), dma((chunks,)), dma((chunks,)),
            dma((tp_n - 1,)), dma((tp_n - 1,)), dma((lat_n - 1,)), dma((lat_n - 1,)),
            dma((lon_n - 1,)), dma((lon_n - 1,)), dma((lat_n - 1,)), dma((lat_n - 1,)),
        ],
        compiler_params=pltpu.CompilerParams(
            collective_id=0, has_side_effects=True, vmem_limit_bytes=60 << 20
        ),
    )(*ins)
    mixed, grad_f, grad_p, grad_step, taps_f, taps_p, logs, bias, gain = pl.pallas_call(
        finish_kernel,
        out_shape=outs,
        in_specs=[VM] * len(outs),
        out_specs=(VM,) * len(outs),
    )(*results)
    return (
        mixed[None], grad_f[None], grad_p[None], grad_step.T[None], taps_f, taps_p, logs,
        bias[0], gain[0],
    )


def solution(mesh):
    in_specs = (
        P("lat", "lon", "tp"),
        P("lat", "lon", None),
        P("lat", "lon", "tp"),
        P("tp"),
        P(None, "tp"),
        P("tp"),
        P(None, "tp"),
        P(),
        P("lat", "tp", None, None),
        P("lat", "tp", None, None),
        P("lat", "lon", "tp"),
    )
    out_specs = (
        P("lat", "lon", "tp"),
        P("lat", "lon", "tp"),
        P("lat", "lon", None),
        P("lat", "lon", "tp"),
        P(None, "tp"),
        P(),
        P(None, "tp"),
        P("tp"),
        P("tp"),
    )
    return jax.shard_map(shards, mesh=mesh, in_specs=in_specs, out_specs=out_specs, check_vma=False)
```

```python
from functools import partial

import jax
import jax.numpy as jnp
from jax import lax
from jax.experimental import pallas as pl
from jax.experimental.pallas import tpu as pltpu
from jax.sharding import PartitionSpec as P

MESH = pl.DeviceIdType.MESH
F32 = jnp.float32
BF16 = jnp.bfloat16
T = 128
EXT = T + 16
CUT = 2
EDGES = ((0, -1), (0, 1), (-1, -1), (-1, 1), (1, -1), (1, 1))


def hi(a, b):
    return jnp.dot(a, b, precision=lax.Precision.HIGHEST, preferred_element_type=F32)


def nn(a, b):
    return jnp.dot(a, b, preferred_element_type=F32)


def nt(a, b):
    return lax.dot_general(a, b, (((1,), (1,)), ((), ())), preferred_element_type=F32)


def tn(a, b):
    return lax.dot_general(a, b, (((0,), (0,)), ((), ())), preferred_element_type=F32)


def grid_peer(d_lat, d_lon):
    lat_n, lon_n = lax.axis_size("lat"), lax.axis_size("lon")
    return {
        "lat": lax.rem(lax.axis_index("lat") + d_lat + lat_n, lat_n),
        "lon": lax.rem(lax.axis_index("lon") + d_lon + lon_n, lon_n),
    }


def greet(peers):
    barrier = pltpu.get_barrier_semaphore()
    for peer in peers:
        pl.semaphore_signal(barrier, inc=1, device_id=peer, device_id_type=MESH)
    pl.semaphore_wait(barrier, len(peers))


def far_first(count):
    return sorted(range(1, count), key=lambda d: -min(d, count - d))


def grid_peers():
    return [grid_peer(a, b) for a in (-1, 0, 1) for b in (-1, 0, 1) if (a, b) != (0, 0)]


def halo_copies(src, lanes, rows, edges, send, recv, base):
    copies = []
    for slot, a in enumerate((-1, 1)):
        copies.append(
            pltpu.make_async_remote_copy(
                src, rows.at[slot, :, lanes], send.at[base + slot], recv.at[base + slot],
                device_id=grid_peer(-a, 0), device_id_type=MESH,
            )
        )
    for slot, (a, b) in enumerate(EDGES):
        part = src.at[pl.ds(T - 16, 16)] if b < 0 else src.at[pl.ds(0, 16)]
        copies.append(
            pltpu.make_async_remote_copy(
                part, edges.at[slot, :, lanes], send.at[base + 2 + slot], recv.at[base + 2 + slot],
                device_id=grid_peer(-a, -b), device_id_type=MESH,
            )
        )
    return copies


def fill_extended(own, lanes, rows, edges, ext):
    lat, lon = lax.axis_index("lat"), lax.axis_index("lon")
    lat_n, lon_n = lax.axis_size("lat"), lax.axis_size("lon")
    keep = {
        (1, -1): (lat > 0).astype(F32),
        (1, 1): (lat < lat_n - 1).astype(F32),
        (2, -1): (lon > 0).astype(F32),
        (2, 1): (lon < lon_n - 1).astype(F32),
    }
    ext[1, 8 : 8 + T, lanes] = own.astype(F32)
    ext[0, 8 : 8 + T, lanes] = rows[0, :, lanes].astype(F32) * keep[1, -1]
    ext[2, 8 : 8 + T, lanes] = rows[1, :, lanes].astype(F32) * keep[1, 1]
    for slot, (a, b) in enumerate(EDGES):
        scale = keep[2, b] if a == 0 else keep[2, b] * keep[1, a]
        tile = edges[slot, :, lanes].astype(F32) * scale
        if b < 0:
            ext[a + 1, 0:8, lanes] = tile[8:16]
        else:
            ext[a + 1, 8 + T :, lanes] = tile[0:8]


def stencil(ext, taps, lanes, adjoint):
    sums = []
    for b in range(3):
        total = None
        for a in range(3):
            term = taps[3 * a + b : 3 * a + b + 1, lanes] * ext[2 - a if adjoint else a, :, lanes]
            total = term if total is None else total + term
        sums.append(total)
    west, east = (sums[2], sums[0]) if adjoint else (sums[0], sums[2])
    full = pltpu.roll(west, 1, 0) + sums[1] + pltpu.roll(east, EXT - 1, 0)
    return full[8 : 8 + T]


def layer_kernel(
    features, projections, cot, raw_r, bias_r, logs_r, gain_r, taps_f, taps_p, start_e, start_w,
    mixed, out_f, out_p, grad_step, out_taps_f, out_taps_p, out_logs, out_bias, out_gain,
    before, active, ext, ext_g, grad_before, taps, rows, edges, rows_g, edges_g,
    add_r, add_l, in_r, in_l, out_r, out_l, dec_r, dec_l, cols, gathered,
    params, by_lat, by_lon, whole,
    send_h, recv_h, send_g, recv_g, send_r, recv_r, send_l, recv_l, send_t, recv_t,
    send_a, recv_a, send_b, recv_b, send_c, recv_c,
):
    lon, tp, lat = lax.axis_index("lon"), lax.axis_index("tp"), lax.axis_index("lat")
    lon_n, tp_n, lat_n = lax.axis_size("lon"), lax.axis_size("tp"), lax.axis_size("lat")
    heads = raw_r.shape[0]
    width = cot.shape[1]
    both = width + projections.shape[1]
    size = width // heads
    split = CUT
    chunks = 2 * heads * split
    tp_peers = [{"tp": lax.rem(tp + d, tp_n)} for d in far_first(tp_n)]
    lat_others = [lax.rem(lat + d, lat_n) for d in far_first(lat_n)]
    lon_others = [lax.rem(lon + d, lon_n) for d in far_first(lon_n)]
    greet(grid_peers() + tp_peers + [{"lat": o} for o in lat_others])
    lanes_f, lanes_p = pl.ds(0, width), pl.ds(width, both - width)
    halo = halo_copies(features, lanes_f, rows, edges, send_h, recv_h, 0)
    halo += halo_copies(projections, lanes_p, rows, edges, send_h, recv_h, 8)
    for copy in halo:
        copy.start()
    taps[:, 0:width] = taps_f[...]
    taps[:, width:both] = taps_p[...]

    row_i = lax.broadcasted_iota(jnp.int32, (T, T), 0)
    col_i = lax.broadcasted_iota(jnp.int32, (T, T), 1)
    lower = (row_i >= col_i).astype(F32)
    upper = (row_i <= col_i).astype(F32)
    spread = (
        lax.broadcasted_iota(jnp.int32, (heads, width), 1) // size
        == lax.broadcasted_iota(jnp.int32, (heads, width), 0)
    ).astype(F32)
    gather = (
        lax.broadcasted_iota(jnp.int32, (width, heads), 0) // size
        == lax.broadcasted_iota(jnp.int32, (width, heads), 1)
    ).astype(F32)

    def softplus(v):
        return jnp.maximum(v, 0.0) + jnp.log1p(jnp.exp(-jnp.abs(v)))

    shifted = raw_r[...].T + bias_r[...]
    steps = softplus(shifted)
    steps_r = steps.T
    rate_e, rate_w = jnp.exp(logs_r[0:1]), jnp.exp(logs_r[1:2])
    sum_e = hi(lower, -steps * rate_e)
    sum_w = hi(upper, -steps * rate_w)
    sum_er, sum_wr = sum_e.T, sum_w.T
    tot_e, tot_w = sum_e[T - 1 : T], sum_w[0:1]
    far_e, far_w = jnp.exp(tot_e - sum_e), jnp.exp(tot_w - sum_w)
    fac_e, fac_w = far_e * steps, far_w * steps
    wide_ee, wide_ew = hi(jnp.exp(sum_e), spread), hi(jnp.exp(sum_w), spread)
    wide_fe, wide_fw = hi(fac_e, spread), hi(fac_w, spread)
    half = heads * split
    close_e = jnp.broadcast_to(jnp.exp(sum_er[:, T - 1 : T]), (heads, T))
    close_w = jnp.broadcast_to(jnp.exp(sum_wr[:, 0:1]), (heads, T))
    for h in range(heads):
        east = jnp.broadcast_to(close_e[h : h + 1], (split, T))
        west = jnp.broadcast_to(close_w[h : h + 1], (split, T))
        dec_r[h * split : (h + 1) * split] = east
        dec_l[h * split : (h + 1) * split] = west
        dec_r[half + h * split : half + (h + 1) * split] = west
        dec_l[half + h * split : half + (h + 1) * split] = east

    gain = hi(jnp.broadcast_to(gain_r[...], (8, heads)), spread)[0:1]

    for copy in halo:
        copy.wait()
    for part in range(both // 128):
        lanes = slice(128 * part, 128 * part + 128)
        if 128 * part < width:
            own = features[:, lanes]
        else:
            own = projections[:, 128 * part - width : 128 * part - width + 128]
        fill_extended(own, lanes, rows, edges, ext)
        value = stencil(ext, taps, lanes, False)
        before[:, lanes] = value
        active[:, lanes] = (value * jax.nn.sigmoid(value)).astype(BF16)

    inner = active[:, 0:width].astype(F32)
    b_part = active[:, width : width + T]
    c_part = active[:, width + T : width + 2 * T]
    incoming = cot[...].astype(F32)
    src_e, src_w = (inner * wide_fe).astype(BF16), (inner * wide_fw).astype(BF16)
    inc_e, inc_w = (incoming * wide_ee).astype(BF16), (incoming * wide_ew).astype(BF16)
    shape3 = (half, size // split, T)
    add_r[0:half] = tn(src_e, b_part).reshape(shape3)
    add_r[half:chunks] = tn(inc_w, c_part).reshape(shape3)
    add_l[0:half] = tn(src_w, b_part).reshape(shape3)
    add_l[half:chunks] = tn(inc_e, c_part).reshape(shape3)

    @pl.when(lon == 0)
    def _():
        in_r[0:half] = start_e[...].reshape(shape3)
        in_r[half:chunks] = jnp.zeros(shape3, F32)

    @pl.when(lon == lon_n - 1)
    def _():
        in_l[0:half] = start_w[...].reshape(shape3)
        in_l[half:chunks] = jnp.zeros(shape3, F32)

    def copy_r(q):
        return pltpu.make_async_remote_copy(
            out_r.at[q], in_r.at[q], send_r.at[q], recv_r.at[q],
            device_id=grid_peer(0, 1), device_id_type=MESH,
        )

    def copy_l(q):
        return pltpu.make_async_remote_copy(
            out_l.at[q], in_l.at[q], send_l.at[q], recv_l.at[q],
            device_id=grid_peer(0, -1), device_id_type=MESH,
        )

    lead = 13
    ahead = 2 * lon - (lon_n - 1)
    skew_r = jnp.clip(ahead * lead, 0, chunks)
    skew_l = jnp.clip(-ahead * lead, 0, chunks)

    def hop(slot, _):
        q_r, q_l = slot - skew_r, slot - skew_l

        @pl.when((q_r >= 0) & (q_r < chunks))
        def _():
            @pl.when(lon > 0)
            def _():
                copy_r(q_r).wait_recv()

            @pl.when(lon < lon_n - 1)
            def _():
                out_r[q_r] = dec_r[pl.ds(q_r, 1), :] * in_r[q_r] + add_r[q_r]
                copy_r(q_r).start()

        @pl.when((q_l >= 0) & (q_l < chunks))
        def _():
            @pl.when(lon < lon_n - 1)
            def _():
                copy_l(q_l).wait_recv()

            @pl.when(lon > 0)
            def _():
                out_l[q_l] = dec_l[pl.ds(q_l, 1), :] * in_l[q_l] + add_l[q_l]
                copy_l(q_l).start()

        return 0

    slots = 2 * chunks
    idle = jnp.abs(ahead) >= (2 * lon_n) // 3
    turn = jnp.where(idle, chunks, slots)
    lax.fori_loop(0, turn, hop, 0)

    scores = nt(c_part, b_part)
    head_i = lax.broadcasted_iota(jnp.int32, (T, heads), 1)
    lane_half = lax.broadcasted_iota(jnp.int32, (T, T), 1) // size
    row_l = jnp.zeros((T, heads), F32)
    row_u = jnp.zeros((T, heads), F32)
    grad_scores = jnp.zeros((T, T), F32)
    per = T // size
    mixes, pulls = [], []
    for pair in range(heads // per):
        lanes = slice(T * pair, T * pair + T)
        inner_p, incoming_p = inner[:, lanes], incoming[:, lanes]
        mix, pull = None, None
        for member in range(per):
            h = per * pair + member
            mine = (lane_half == member).astype(F32)
            inner_m = (inner_p * mine).astype(BF16)
            incoming_m = (incoming_p * mine).astype(BF16)
            gap = jnp.where(
                row_i >= col_i,
                sum_e[:, h : h + 1] - sum_er[h : h + 1],
                sum_w[:, h : h + 1] - sum_wr[h : h + 1],
            )
            decay = jnp.where(row_i == col_i, 2.0, jnp.exp(gap)) * steps_r[h : h + 1]
            grad_mix = nt(incoming_m, inner_m) * decay
            grad_scores = grad_scores + grad_mix
            weight = grad_mix * scores
            below = jnp.where(row_i > col_i, weight, 0.0)
            above = jnp.where(row_i < col_i, weight, 0.0)
            row_l = jnp.where(head_i == h, jnp.sum(below, axis=1, keepdims=True), row_l)
            row_u = jnp.where(head_i == h, jnp.sum(above, axis=1, keepdims=True), row_u)
            cols[0, h : h + 1] = jnp.sum(below, axis=0, keepdims=True)
            cols[1, h : h + 1] = jnp.sum(above, axis=0, keepdims=True)
            cols[2, h : h + 1] = jnp.sum(weight, axis=0, keepdims=True)
            mixing = (decay * scores).astype(BF16)
            y, g = nn(mixing, inner_m), tn(mixing, incoming_m)
            mix = y if mix is None else mix + y
            pull = g if pull is None else pull + g
        mixes.append(mix)
        pulls.append(pull)
    grad_inner = jnp.concatenate(pulls, axis=1)
    total = jnp.concatenate(mixes, axis=1)

    lax.fori_loop(turn, slots, hop, 0)

    flat = (width, T)
    ent_e, adj_w = in_r[0:half].reshape(flat), in_r[half:chunks].reshape(flat)
    ent_w, adj_e = in_l[0:half].reshape(flat), in_l[half:chunks].reshape(flat)
    ent_eb, ent_wb = ent_e.astype(BF16), ent_w.astype(BF16)
    adj_eb, adj_wb = adj_e.astype(BF16), adj_w.astype(BF16)

    scores_b = grad_scores.astype(BF16)
    me = pl.ds(tp, 1)
    scores_t = (grad_scores - scores_b.astype(F32)).astype(BF16)

    def low(value, rounded):
        return (value - rounded.astype(F32)).astype(BF16)

    grad_b = (
        tn(scores_b, c_part) + tn(scores_t, c_part)
        + nn(src_e, adj_eb) + nn(src_e, low(adj_e, adj_eb))
        + nn(src_w, adj_wb) + nn(src_w, low(adj_w, adj_wb))
    )
    grad_c = (
        nn(scores_b, b_part) + nn(scores_t, b_part)
        + nn(inc_e, ent_eb) + nn(inc_e, low(ent_e, ent_eb))
        + nn(inc_w, ent_wb) + nn(inc_w, low(ent_w, ent_wb))
    )
    gathered[me, :, 0:T] = grad_b.astype(BF16)[None]
    gathered[me, :, T : 2 * T] = grad_c.astype(BF16)[None]
    copies = [
        pltpu.make_async_remote_copy(
            gathered.at[tp], gathered.at[tp], send_t.at[d], recv_t.at[d],
            device_id=peer, device_id_type=MESH,
        )
        for d, peer in enumerate(tp_peers)
    ]
    for copy in copies:
        copy.start()

    read_e = nt(c_part, ent_eb) * wide_ee
    read_w = nt(c_part, ent_wb) * wide_ew
    pull_e, pull_w = nt(b_part, adj_eb), nt(b_part, adj_wb)
    mixed[...] = (total + read_e + read_w + gain * inner).astype(BF16)
    grad_inner = grad_inner + wide_fe * pull_e + wide_fw * pull_w + gain * incoming
    r_e, r_w = hi(read_e * incoming, gather), hi(read_w * incoming, gather)
    q_e, q_w = hi(pull_e * inner, gather), hi(pull_w * inner, gather)
    ones = jnp.ones((8, T), F32)

    def per_head(v):
        return lax.dot_general(
            ones, hi(spread, v), (((1,), (1,)), ((), ())),
            precision=lax.Precision.HIGHEST, preferred_element_type=F32,
        )[0:1]

    end_e, end_w = per_head(adj_e * ent_e), per_head(adj_w * ent_w)
    w_e, w_w = fac_e * q_e, fac_w * q_w
    const_e = jnp.sum(w_e, axis=0, keepdims=True) + jnp.exp(tot_e) * end_e
    const_w = jnp.sum(w_w, axis=0, keepdims=True) + jnp.exp(tot_w) * end_w
    grad_log_e = hi(upper, row_l - cols[0].T + r_e - w_e) + const_e
    grad_log_w = hi(lower, row_u - cols[1].T + r_w - w_w) + const_w
    grad_steps = (
        (cols[2] / steps_r).T + far_e * q_e + far_w * q_w - rate_e * grad_log_e - rate_w * grad_log_w
    )
    grad_raw = grad_steps * jax.nn.sigmoid(shifted)
    grad_step[...] = grad_raw.T
    small = both // 128
    params[small:8] = jnp.zeros((8 - small, 8, 128), F32)
    params[small + 1, 0:1, 0:heads] = jnp.sum(-steps * rate_e * grad_log_e, axis=0, keepdims=True)
    params[small + 1, 1:2, 0:heads] = jnp.sum(-steps * rate_w * grad_log_w, axis=0, keepdims=True)
    params[small + 1, 2:3, 0:heads] = jnp.sum(grad_raw, axis=0, keepdims=True)
    params[small + 1, 3:4, 0:heads] = jnp.sum(hi(incoming * inner, gather), axis=0, keepdims=True)

    def back(part, grad_active):
        lanes = slice(128 * part, 128 * part + 128)
        value = before[:, lanes]
        slope = jax.nn.sigmoid(value)
        grad = (
            grad_active.astype(BF16).astype(F32) * slope * (1.0 + value * (1.0 - slope))
        ).astype(BF16)
        grad_before[:, lanes] = grad

    def weigh(part):
        lanes = slice(128 * part, 128 * part + 128)
        edge = jnp.zeros((8, 128), F32)
        wide = jnp.concatenate([edge, grad_before[:, lanes].astype(F32), edge], axis=0)
        for b in range(3):
            moved = wide if b == 1 else pltpu.roll(wide, EXT - 1 if b == 0 else 1, 0)
            for a in range(3):
                tap = jnp.sum(moved * ext[a, :, lanes], axis=0, keepdims=True)
                if 3 * a + b < 8:
                    params[part, 3 * a + b : 3 * a + b + 1] = tap
                else:
                    params[small, part : part + 1] = tap

    parts_f = width // 128
    for part in range(parts_f):
        back(part, grad_inner[:, 128 * part : 128 * part + 128])
    halo_f = halo_copies(grad_before.at[:, lanes_f], lanes_f, rows_g, edges_g, send_g, recv_g, 0)
    for copy in halo_f:
        copy.start()
    for part in range(parts_f):
        weigh(part)
    for copy in copies:
        copy.wait()
    proj = gathered[0].astype(F32)
    for d in range(1, tp_n):
        proj = proj + gathered[d].astype(F32)
    for part in range(2):
        back(parts_f + part, proj[:, 128 * part : 128 * part + 128])
    halo_p = halo_copies(grad_before.at[:, lanes_p], lanes_p, rows_g, edges_g, send_g, recv_g, 8)
    for copy in halo_p:
        copy.start()
    for part in range(2):
        weigh(parts_f + part)

    per_lat = 8 // lat_n
    mine = pl.ds(lat * per_lat, per_lat)
    share = [
        pltpu.make_async_remote_copy(
            params.at[pl.ds(other * per_lat, per_lat)], by_lat.at[lat], send_a.at[d], recv_a.at[d],
            device_id={"lat": other}, device_id_type=MESH,
        )
        for d, other in enumerate(lat_others)
    ]
    for copy in share:
        copy.start()
    by_lat[pl.ds(lat, 1)] = params[mine][None]

    def adjoint(part):
        lanes = slice(128 * part, 128 * part + 128)
        fill_extended(grad_before[:, lanes], lanes, rows_g, edges_g, ext_g)
        value = stencil(ext_g, taps, lanes, True).astype(BF16)
        if part < parts_f:
            out_f[:, lanes] = value
        else:
            out_p[:, 128 * part - width : 128 * part - width + 128] = value

    for copy in share:
        copy.wait()
    sums = by_lat[0]
    for d in range(1, lat_n):
        sums = sums + by_lat[d]
    by_lon[pl.ds(lon, 1)] = sums[None]
    share = [
        pltpu.make_async_remote_copy(
            by_lon.at[lon], by_lon.at[lon], send_b.at[d], recv_b.at[d],
            device_id={"lon": other}, device_id_type=MESH,
        )
        for d, other in enumerate(lon_others)
    ]
    for copy in share:
        copy.start()
    for copy in halo_f + halo_p:
        copy.wait()
    for part in range(both // 128):
        adjoint(part)
    for copy in share:
        copy.wait()
    sums = by_lon[0]
    for d in range(1, lon_n):
        sums = sums + by_lon[d]
    cells = T * lat_n * lon_n
    whole[pl.ds(lat, 1)] = (sums * cells ** (-0.5))[None]
    share = [
        pltpu.make_async_remote_copy(
            whole.at[lat], whole.at[lat], send_c.at[d], recv_c.at[d],
            device_id={"lat": other}, device_id_type=MESH,
        )
        for d, other in enumerate(lat_others)
    ]
    for copy in share:
        copy.start()

    def settle(q, _):
        @pl.when(lon < lon_n - 1)
        def _():
            copy_r(q).wait_send()

        @pl.when(lon > 0)
        def _():
            copy_l(q).wait_send()

        return 0

    lax.fori_loop(0, chunks, settle, 0)

    for copy in share:
        copy.wait()
    for part in range(both // 128):
        tile = whole[part // per_lat, part % per_lat]
        last = whole[small // per_lat, small % per_lat, part : part + 1]
        target = out_taps_f if part < parts_f else out_taps_p
        lanes = slice(128 * (part % parts_f), 128 * (part % parts_f) + 128)
        target[0:8, lanes] = tile
        target[8:9, lanes] = last
    tile = whole[(small + 1) // per_lat, (small + 1) % per_lat]
    out_logs[...] = tile[0:2, 0:heads]
    out_bias[...] = tile[2:3, 0:heads]
    out_gain[...] = tile[3:4, 0:heads]


def finish_kernel(*refs):
    count = len(refs) // 2
    for source, target in zip(refs[:count], refs[count:]):
        target[...] = source[...]


VM = pl.BlockSpec(memory_space=pltpu.VMEM)


def shards(
    features, projections, step_raw, step_bias, decay_log, skip_gain, conv_features,
    conv_projections, state_east, state_west, cotangent,
):
    width, heads = features.shape[2], step_raw.shape[2]
    extra = projections.shape[2]
    both = width + extra
    tp_n, lat_n, lon_n = lax.axis_size("tp"), lax.axis_size("lat"), lax.axis_size("lon")
    sds = jax.ShapeDtypeStruct
    dma = pltpu.SemaphoreType.DMA
    vm = pltpu.VMEM
    flat = (width, T)
    chunks = 2 * heads * CUT
    block = vm((chunks, width // heads // CUT, T), F32)
    outs = (
        sds((T, width), BF16), sds((T, width), BF16), sds((T, extra), BF16), sds((heads, T), F32),
        sds((9, width), F32), sds((9, extra), F32), sds((2, heads), F32), sds((1, heads), F32),
        sds((1, heads), F32),
    )
    ins = (
        features[0], projections[0], cotangent[0], step_raw[0].T, step_bias[None], decay_log,
        skip_gain[None], conv_features, conv_projections, state_east.reshape(flat),
        state_west.reshape(flat),
    )
    per_lat = 8 // lat_n
    results = pl.pallas_call(
        layer_kernel,
        out_shape=outs,
        in_specs=[VM] * len(ins),
        out_specs=(VM,) * len(outs),
        scratch_shapes=[
            vm((T, both), F32), vm((T, both), BF16), vm((3, EXT, both), F32), vm((3, EXT, both), F32),
            vm((T, both), BF16), vm((9, both), F32),
            vm((2, T, both), BF16), vm((6, 16, both), BF16),
            vm((2, T, both), BF16), vm((6, 16, both), BF16),
            block, block, block, block, block, block,
            vm((chunks, T), F32), vm((chunks, T), F32), vm((3, heads, T), F32),
            vm((tp_n, T, extra), BF16),
            vm((8, 8, 128), F32), vm((lat_n, per_lat, 8, 128), F32),
            vm((lon_n, per_lat, 8, 128), F32), vm((lat_n, per_lat, 8, 128), F32),
            dma((16,)), dma((16,)), dma((16,)), dma((16,)),
            dma((chunks,)), dma((chunks,)), dma((chunks,)), dma((chunks,)),
            dma((tp_n - 1,)), dma((tp_n - 1,)), dma((lat_n - 1,)), dma((lat_n - 1,)),
            dma((lon_n - 1,)), dma((lon_n - 1,)), dma((lat_n - 1,)), dma((lat_n - 1,)),
        ],
        compiler_params=pltpu.CompilerParams(
            collective_id=0, has_side_effects=True, vmem_limit_bytes=60 << 20
        ),
    )(*ins)
    mixed, grad_f, grad_p, grad_step, taps_f, taps_p, logs, bias, gain = pl.pallas_call(
        finish_kernel,
        out_shape=outs,
        in_specs=[VM] * len(outs),
        out_specs=(VM,) * len(outs),
    )(*results)
    return (
        mixed[None], grad_f[None], grad_p[None], grad_step.T[None], taps_f, taps_p, logs,
        bias[0], gain[0],
    )


def solution(mesh):
    in_specs = (
        P("lat", "lon", "tp"),
        P("lat", "lon", None),
        P("lat", "lon", "tp"),
        P("tp"),
        P(None, "tp"),
        P("tp"),
        P(None, "tp"),
        P(),
        P("lat", "tp", None, None),
        P("lat", "tp", None, None),
        P("lat", "lon", "tp"),
    )
    out_specs = (
        P("lat", "lon", "tp"),
        P("lat", "lon", "tp"),
        P("lat", "lon", None),
        P("lat", "lon", "tp"),
        P(None, "tp"),
        P(),
        P(None, "tp"),
        P("tp"),
        P("tp"),
    )
    return jax.shard_map(shards, mesh=mesh, in_specs=in_specs, out_specs=out_specs, check_vma=False)
```
